32 devices in a mesh: tiles: 2 (over y), pat: 16 (over z, x, core).
Axes of the slice: x: 2, y: 2, z: 4, core: 2. Of those that a mesh axis runs over, the one named last changes fastest.
Arguments:
- slab_phase: float32 [6, 1024, 1024], P('tiles', 'pat'), parts along dimension 0, may hold values from -2 to 2
- pupil_phase: float32 [1024, 1024], P('pat'), may hold values from -5 to 5
- pupil_mask: int32 [1024, 1024], P('pat'), may hold values from 0 to 1, as said below
- led_code: int32 [4, 2], replicated, may hold values from 0 to 1, as said below
- led_freq: int32 [2, 2], replicated, may hold values from -32 to 32
- measured: int32 [8, 1024, 1024], P('tiles', 'pat'), parts along dimension 0, may hold values from 1 to 2048
Outputs:
- phase_grad: float32 [6, 1024, 1024], P('tiles', 'pat'), parts along dimension 0
The draws below stay inside these ranges and needn't reach their ends.
There are 2 independent parts, one for each index of `tiles`. The reference program is written for one: setup_inputs(seed, part) draws one part's arguments, and reference() takes and returns one part's arrays. A program takes and returns all parts, laid end to end along the dimension named above; an argument that names none is the same for every part. Nothing has to cross between parts.
Inputs may be any that keep to these rules, and one draw needn't show every extreme that they name: `pupil_mask`: 1 at every frequency pair with freq(u)^2 + freq(v)^2 <= 9216, 0 where it is >= 16384, either value between. `led_code`: pattern p always has LED p mod 2 switched on.
All inputs are finite; a program needn't handle non-finite values.
Results may differ from the reference program's by a relative error of at most 0.0003.
Values sent between devices are 32-bit elements; how exact they have to be, the bound alone decides.
A program may use at most 128 MiB of HBM per device.

```python
import math
import jax
import jax.numpy as jnp
from jax import lax

N = 1024
SLICES = 3
LEDS = 2
PATTERNS = 4
PUP_OUT = 128
PUP_IN = 96
LED_MAX = 32


def draw_pupil_mask(key, part):
    grid_index = jnp.arange(N, dtype=jnp.int32)
    frequency_index = (grid_index + N // 2) % N - N // 2
    radius = frequency_index[:, None] * frequency_index[:, None] + frequency_index[None, :] * frequency_index[None, :]
    coin_flip = jax.random.randint(key, (N, N), 0, 2, dtype=jnp.int32)
    opened = jnp.where(radius <= PUP_IN * PUP_IN, 1, coin_flip)
    return jnp.where(radius >= PUP_OUT * PUP_OUT, 0, opened).astype(jnp.int32)


def draw_led_code(key, part):
    coin_flip = jax.random.randint(key, (PATTERNS, LEDS), 0, 2, dtype=jnp.int32)
    pattern_index = jnp.arange(PATTERNS, dtype=jnp.int32)[:, None] % LEDS
    forced = (pattern_index == jnp.arange(LEDS, dtype=jnp.int32)[None, :]).astype(jnp.int32)
    return jnp.maximum(coin_flip, forced).astype(jnp.int32)


def draw_measured(key, part):
    level_key, count_key = jax.random.split(key)
    row_level = jnp.arange(N, dtype=jnp.int32) * 4 // N
    col_level = jax.random.randint(level_key, (N,), 0, 4, dtype=jnp.int32)
    ceiling = jnp.left_shift(jnp.int32(32), row_level[:, None] + col_level[None, :])
    return jax.random.randint(count_key, (PATTERNS, N, N), 1, ceiling[None, :, :] + 1, dtype=jnp.int32)


def set_ends(entries, stream_key, low, largest):
    spot = [jax.random.randint(jax.random.fold_in(stream_key, axis), (), 0, length) for axis, length in enumerate(entries.shape)]
    widest = entries.shape.index(max(entries.shape))
    beside = spot[:widest] + [(spot[widest] + 1) % entries.shape[widest]] + spot[widest + 1:]
    return entries.at[tuple(spot)].set(low).at[tuple(beside)].set(largest)


def block_scale(rng, extent, shards, smallest, top_value):
    factor_of, own = 1.0, jax.random.fold_in(rng, 6)
    for position, blocks in shards:
        heights = jnp.exp(jax.random.uniform(jax.random.fold_in(own, position), (blocks,), jnp.float32, smallest / len(shards), top_value / len(shards)))
        factor_of = factor_of * jnp.repeat(heights, extent[position] // blocks).reshape([-1 if axis == position else 1 for axis in range(len(extent))])
    return factor_of


def scatter_about(rng, shape, deviation, limit, shards=(), held_as=jnp.bfloat16):
    gain = block_scale(rng, shape, shards, -0.22, 0.18) if shards else 1.0
    entries = jax.random.normal(rng, shape, jnp.float32) * deviation * gain
    return jnp.minimum(jnp.maximum(entries, -limit), limit).astype(held_as)


def setup_inputs(seed: int = 0, part: int = 0) -> dict:
    arg_keys = jax.random.split(jax.random.key(seed), 7)
    own_keys = jax.random.split(jax.random.fold_in(arg_keys[6], part), 7)
    return {
        "slab_phase": jnp.clip(jax.random.uniform(own_keys[0], (SLICES, N, N), jnp.float32, -2.0, 2.0) * block_scale(own_keys[0], (SLICES, N, N), ((1, 16),), -0.4, 0.0), -2.0, 2.0),
        "pupil_phase": scatter_about(arg_keys[1], (N, N), 1.0, 5.0, ((0, 16),), jnp.float32),
        "pupil_mask": draw_pupil_mask(jax.random.fold_in(arg_keys[6], 71), part),
        "led_code": draw_led_code(jax.random.fold_in(arg_keys[6], 71), part),
        "led_freq": set_ends(jax.random.randint(arg_keys[4], (LEDS, 2), 0 - LED_MAX, LED_MAX + 1), jax.random.fold_in(arg_keys[4], 1), 0 - LED_MAX, LED_MAX).astype(jnp.int32),
        "measured": draw_measured(jax.random.fold_in(jax.random.fold_in(arg_keys[6], part), 71), part),
    }


spread_rate = 0.3
highest = lax.Precision.HIGHEST

def frequency(grid_index, grid_size):
    return (grid_index + grid_size // 2) % grid_size - grid_size // 2

def fourier(values):
    return jnp.fft.fft2(values, norm='ortho')

def inverse(values):
    return jnp.fft.ifft2(values, norm='ortho')

def reference(slab_phase, pupil_phase, pupil_mask, led_code, led_freq, measured):
    grid_index = jnp.arange(N, dtype=jnp.int32)
    spatial = frequency(grid_index, N)
    radius = spatial[:, None] * spatial[:, None] + spatial[None, :] * spatial[None, :]
    cutoff = N // 2 * (N // 2)
    inside = radius <= cutoff
    height = jnp.sqrt(jnp.maximum(cutoff - radius, 0).astype(jnp.float32))
    phase_shift = spread_rate * (height - N // 2)
    propagator = jnp.where(inside, jnp.cos(phase_shift), 0.0) + 1j * jnp.where(inside, jnp.sin(phase_shift), 0.0)
    opening = pupil_mask.T.astype(jnp.float32)
    pupil = opening * jnp.cos(pupil_phase.T) + 1j * (opening * jnp.sin(pupil_phase.T))
    tilt_index = (led_freq[:, 0][:, None, None] * grid_index[None, :, None] + led_freq[:, 1][:, None, None] * grid_index[None, None, :]) % N
    tilt_angle = tilt_index.astype(jnp.float32) * (2.0 * math.pi / N)
    wave_field = jnp.cos(tilt_angle) + 1j * jnp.sin(tilt_angle)
    transmission = jnp.cos(slab_phase) + 1j * jnp.sin(slab_phase)
    passed_list = []
    for slab_index in range(SLICES):
        passed = wave_field * transmission[slab_index][None]
        passed_list.append(passed)
        spectral_factor = propagator if slab_index < SLICES - 1 else pupil
        wave_field = inverse(spectral_factor[None] * fourier(passed))
    camera = wave_field
    led_power = jnp.real(camera) * jnp.real(camera) + jnp.imag(camera) * jnp.imag(camera)
    code_float = led_code.astype(jnp.float32)
    pattern_power = jnp.einsum('pl,lrc->prc', code_float, led_power, precision=highest)
    counts = measured.astype(jnp.float32)
    area = float(N * N)
    mean_power = lax.optimization_barrier(jnp.sum(pattern_power, axis=(1, 2))) / area
    mean_count = lax.optimization_barrier(jnp.sum(counts, axis=(1, 2))) / area
    relative = pattern_power / mean_power[:, None, None]
    misfit = relative - counts / mean_count[:, None, None]
    coupling = lax.optimization_barrier(jnp.sum(misfit * relative, axis=(1, 2))) / area
    pattern_weight = (misfit - coupling[:, None, None]) / mean_power[:, None, None]
    led_weight = jnp.einsum('pl,prc->lrc', code_float, pattern_weight, precision=highest)
    adjoint_field = 2.0 * led_weight * camera
    back_field = inverse(jnp.conj(pupil)[None] * fourier(adjoint_field))
    gradients = [None] * SLICES
    for slab_index in range(SLICES - 1, -1, -1):
        gradients[slab_index] = lax.optimization_barrier(jnp.sum(jnp.imag(jnp.conj(passed_list[slab_index]) * back_field), axis=0))
        if slab_index > 0:
            released = back_field * jnp.conj(transmission[slab_index])[None]
            back_field = inverse(jnp.conj(propagator)[None] * fourier(released))
    return jnp.stack(gradients)
```

```python
import functools
import math
import types

import jax
import jax.numpy as jnp
import numpy as np
from jax import lax
from jax.experimental import pallas as pl
from jax.experimental.pallas import tpu as pltpu
from jax.sharding import PartitionSpec as P

spread_rate = 0.3
highest = lax.Precision.HIGHEST


def frequency(grid_index, grid_size):
    return (grid_index + grid_size // 2) % grid_size - grid_size // 2


def complex_times(values, factor):
    real_part = values[0] * factor[0] - values[1] * factor[1]
    imag_part = values[0] * factor[1] + values[1] * factor[0]
    return jnp.stack([real_part, imag_part])


def dft_block(length, direction, norm_factor):
    grid_index = jnp.arange(length, dtype=jnp.int32)
    angles = (grid_index[:, None] * grid_index[None, :] % length).astype(jnp.float32) * (
        2.0 * math.pi / length
    )
    cosine = jnp.cos(angles) * norm_factor
    signed_sine = direction * jnp.sin(angles) * norm_factor
    real_rows = jnp.stack([cosine, signed_sine], 1)
    imag_rows = jnp.stack([-signed_sine, cosine], 1)
    return jnp.stack([real_rows, imag_rows], 0)


def twiddle_table(short_size, long_size, grid_size, direction):
    short_index = jnp.arange(short_size, dtype=jnp.int32)
    long_index = jnp.arange(long_size, dtype=jnp.int32)
    angles = (short_index[:, None] * long_index[None, :] % grid_size).astype(jnp.float32) * (
        2.0 * math.pi / grid_size
    )
    return jnp.stack([jnp.cos(angles), direction * jnp.sin(angles)])


def table_set(col_count, dev_count, grid_size, direction):
    short_table = dft_block(col_count, direction, 1.0)
    long_table = dft_block(dev_count, direction, 1.0 / math.sqrt(grid_size))
    return (short_table, long_table, twiddle_table(col_count, dev_count, grid_size, direction))


def to_fourier(wave_field, tables, dev_count):
    short_table, long_table, twiddles = tables
    led_count = wave_field.shape[1]
    row_count = wave_field.shape[2]
    grid_size = wave_field.shape[3]
    col_count = grid_size // dev_count
    shaped = wave_field.reshape(2, led_count, row_count, col_count, dev_count)
    sectioned = jnp.einsum("zlrmq,zmwc->wlrcq", shaped, short_table, precision=highest)
    sectioned = complex_times(sectioned, twiddles)
    outgoing = jnp.einsum("wlrcq,wqvd->dvlcr", sectioned, long_table, precision=highest)
    incoming = lax.all_to_all(
        outgoing.reshape(dev_count, -1), "pat", split_axis=0, concat_axis=0, tiled=True
    )
    incoming = incoming.reshape(dev_count, 2, led_count, col_count, row_count)
    sectioned = jnp.einsum("swlcr,wsvj->vlcrj", incoming, long_table, precision=highest)
    sectioned = complex_times(sectioned, twiddles)
    sectioned = jnp.einsum("wlcrj,wrvh->vlchj", sectioned, short_table, precision=highest)
    return sectioned.reshape(2, led_count, col_count, grid_size)


def to_space(spectrum, tables, dev_count):
    short_table, long_table, twiddles = tables
    led_count = spectrum.shape[1]
    col_count = spectrum.shape[2]
    grid_size = spectrum.shape[3]
    row_count = grid_size // dev_count
    shaped = spectrum.reshape(2, led_count, col_count, row_count, dev_count)
    sectioned = jnp.einsum("zlcmq,zmwr->wlcrq", shaped, short_table, precision=highest)
    sectioned = complex_times(sectioned, twiddles)
    outgoing = jnp.einsum("wlcrq,wqvd->dvlcr", sectioned, long_table, precision=highest)
    incoming = lax.all_to_all(
        outgoing.reshape(dev_count, -1), "pat", split_axis=0, concat_axis=0, tiled=True
    )
    incoming = incoming.reshape(dev_count, 2, led_count, col_count, row_count)
    sectioned = jnp.einsum("swlcr,wsvj->vlrcj", incoming, long_table, precision=highest)
    sectioned = complex_times(sectioned, twiddles)
    sectioned = jnp.einsum("wlrcj,wcvh->vlrhj", sectioned, short_table, precision=highest)
    return sectioned.reshape(2, led_count, row_count, grid_size)


def plain_body(slab_phase, pupil_phase, pupil_mask, led_code, led_freq, measured):
    dev_count = lax.axis_size("pat")
    position = lax.axis_index("pat")
    slab_count, row_count, grid_size = slab_phase.shape
    col_count = grid_size // dev_count
    pattern_count, led_count = led_code.shape
    area = float(grid_size * grid_size)
    forward_set = table_set(col_count, dev_count, grid_size, -1.0)
    inverse_set = table_set(col_count, dev_count, grid_size, 1.0)
    conjugate = jnp.array([1.0, -1.0], jnp.float32)[:, None, None]
    col_freq = frequency(position * col_count + jnp.arange(col_count, dtype=jnp.int32), grid_size)
    row_freq = frequency(jnp.arange(grid_size, dtype=jnp.int32), grid_size)
    radius = col_freq[:, None] * col_freq[:, None] + row_freq[None, :] * row_freq[None, :]
    cutoff = grid_size // 2 * (grid_size // 2)
    inside = radius <= cutoff
    height = jnp.sqrt(jnp.maximum(cutoff - radius, 0).astype(jnp.float32))
    phase_shift = spread_rate * (height - grid_size // 2)
    propagator = jnp.stack(
        [jnp.where(inside, jnp.cos(phase_shift), 0.0), jnp.where(inside, jnp.sin(phase_shift), 0.0)]
    )
    opening = pupil_mask.astype(jnp.float32)
    pupil = jnp.stack([opening * jnp.cos(pupil_phase), opening * jnp.sin(pupil_phase)])
    propagator_conj = propagator * conjugate
    pupil_conj = pupil * conjugate
    row_index = position * row_count + jnp.arange(row_count, dtype=jnp.int32)
    col_index = jnp.arange(grid_size, dtype=jnp.int32)
    tilt_index = (
        led_freq[:, 0][:, None, None] * row_index[None, :, None]
        + led_freq[:, 1][:, None, None] * col_index[None, None, :]
    ) % grid_size
    tilt_angle = tilt_index.astype(jnp.float32) * (2.0 * math.pi / grid_size)
    illumination = jnp.stack([jnp.cos(tilt_angle), jnp.sin(tilt_angle)])
    transmission = jnp.stack([jnp.cos(slab_phase), jnp.sin(slab_phase)])
    group_count = 1
    group_size = led_count // group_count
    wave_groups = [illumination]
    passed_groups = []
    for slab_index in range(slab_count):
        factor = transmission[:, slab_index]
        passed = [complex_times(wave_field, factor) for wave_field in wave_groups]
        passed_groups.append(passed)
        spectral_factor = propagator if slab_index < slab_count - 1 else pupil
        wave_groups = [
            to_space(
                complex_times(to_fourier(passed_field, forward_set, dev_count), spectral_factor),
                inverse_set,
                dev_count,
            )
            for passed_field in passed
        ]
    camera = wave_groups[0]
    led_power = camera[0] * camera[0] + camera[1] * camera[1]
    code_float = led_code.astype(jnp.float32)
    pattern_power = jnp.dot(
        code_float, led_power.reshape(led_count, -1), precision=highest
    ).reshape(pattern_count, row_count, grid_size)
    counts = measured.astype(jnp.float32)
    power_sum, count_sum = lax.psum(
        (jnp.sum(pattern_power, axis=(1, 2)), jnp.sum(counts, axis=(1, 2))), "pat"
    )
    mean_power = power_sum / area
    mean_count = count_sum / area
    relative = pattern_power / mean_power[:, None, None]
    misfit = relative - counts / mean_count[:, None, None]
    coupling = lax.psum(jnp.sum(misfit * relative, axis=(1, 2)), "pat") / area
    pattern_weight = (misfit - coupling[:, None, None]) / mean_power[:, None, None]
    led_weight = jnp.dot(
        code_float.T, pattern_weight.reshape(pattern_count, -1), precision=highest
    ).reshape(led_count, row_count, grid_size)
    camera_adjoint = 2.0 * led_weight[None] * camera
    adjoint_groups = [camera_adjoint]
    gradients = [None] * slab_count
    for slab_index in range(slab_count - 1, -1, -1):
        spectral_factor = pupil_conj if slab_index == slab_count - 1 else propagator_conj
        back_groups = [
            to_space(
                complex_times(to_fourier(adjoint_field, forward_set, dev_count), spectral_factor),
                inverse_set,
                dev_count,
            )
            for adjoint_field in adjoint_groups
        ]
        gradient = jnp.zeros((row_count, grid_size), jnp.float32)
        for passed_field, back_field in zip(passed_groups[slab_index], back_groups):
            gradient = jnp.sum(
                passed_field[0] * back_field[1] - passed_field[1] * back_field[0], axis=0
            )
        gradients[slab_index] = gradient
        if slab_index > 0:
            release = transmission[:, slab_index] * conjugate
            adjoint_groups = [complex_times(back_field, release) for back_field in back_groups]
    return jnp.stack(gradients)


class Names(types.SimpleNamespace):
    pass


pupil_radius = 128
lanes = 128
f32 = jnp.float32
bf16 = jnp.bfloat16


def halves(table):
    table32 = np.asarray(table, np.float32)
    high = table32.astype(bf16)
    low = (table32 - high.astype(np.float32)).astype(bf16)
    return np.stack([high, low])


def row_tables(size, block, band_block):
    quarter = size // 4
    pos = np.arange(quarter)
    angle = 2.0 * np.pi * ((pos[:, None] * pos[None, :]) % quarter) / quarter
    cosine = np.cos(angle) / math.sqrt(size)
    sine = np.sin(angle) / math.sqrt(size)

    def forward(freqs, width):
        parts = []
        for first in range(0, len(freqs), width):
            pick = freqs[first : first + width] % quarter
            left = np.concatenate([cosine[:, pick], sine[:, pick]], 0)
            right = np.concatenate([-sine[:, pick], cosine[:, pick]], 0)
            parts.append(np.concatenate([left, right], 1))
        return np.concatenate(parts, 1)

    full = forward(pos, block)
    reach = pupil_radius // 4
    band = forward(np.arange(-reach, reach), band_block)
    theta = 2.0 * np.pi * (np.arange(4)[:, None] * pos[None, :]) / size
    twiddle = np.concatenate([np.cos(theta), np.sin(theta)], 0).astype(np.float32)
    return Names(
        full=jnp.asarray(halves(full)),
        full_inv=jnp.asarray(halves(full.T)),
        band=jnp.asarray(halves(band)),
        band_inv=jnp.asarray(halves(band.T)),
        twiddle=jnp.asarray(twiddle),
    )


def col_tables(size):
    quarter = size // 4
    pos = np.arange(quarter)
    angle = 2.0 * np.pi * ((pos[:, None] * pos[None, :]) % quarter) / quarter
    both = np.concatenate([np.cos(angle), np.sin(angle)], 0) / math.sqrt(size)
    theta = 2.0 * np.pi * (np.arange(1, 4)[:, None] * pos[None, :]) / size
    twiddle = np.stack([np.cos(theta), np.sin(theta)]).astype(np.float32)
    twiddle = np.ascontiguousarray(np.broadcast_to(twiddle[..., None], twiddle.shape + (lanes,)))
    freqs = np.arange(-pupil_radius, pupil_radius)
    angle = 2.0 * np.pi * ((np.arange(size)[:, None] * freqs[None, :]) % size) / size
    cosine = np.cos(angle) / math.sqrt(size)
    sine = np.sin(angle) / math.sqrt(size)
    band = halves(np.concatenate([cosine, sine], 1))
    band_inv = halves(np.concatenate([cosine.T, sine.T], 1))
    return Names(both=halves(both), twiddle=twiddle, band=band, band_inv=band_inv)


def split(value):
    high = value.astype(bf16)
    return high, (value - high.astype(f32)).astype(bf16)


def dot3(left, right):
    def dot(a, b):
        return jnp.dot(a, b, preferred_element_type=f32)

    return dot(left[0], right[0]) + (dot(left[0], right[1]) + dot(left[1], right[0]))


def turn(value):
    rolled = pltpu.roll(value, lanes // 2, 1)
    lane = lax.broadcasted_iota(jnp.int32, value.shape, 1)
    return jnp.where(lane < lanes // 2, rolled, -rolled)


def row_spread(blocks, twiddle_ref):
    (r0, i0), (r1, i1), (r2, i2), (r3, i3) = blocks
    sr, si, tr, ti = r0 + r2, i0 + i2, r1 + r3, i1 + i3
    dr, di, er, ei = r0 - r2, i0 - i2, r1 - r3, i1 - i3
    mixed = [(sr + tr, si + ti), (dr + ei, di - er), (sr - tr, si - ti), (dr - ei, di + er)]
    out = [mixed[0]]
    for j in range(1, 4):
        cosine, sine = twiddle_ref[j : j + 1, :], twiddle_ref[4 + j : 5 + j, :]
        re, im = mixed[j]
        out.append((re * cosine + im * sine, im * cosine - re * sine))
    return out


def row_gather(parts, twiddle_ref):
    g = [parts[0]]
    for j in range(1, 4):
        cosine, sine = twiddle_ref[j : j + 1, :], twiddle_ref[4 + j : 5 + j, :]
        re, im = parts[j]
        g.append((re * cosine - im * sine, im * cosine + re * sine))
    (r0, i0), (r1, i1), (r2, i2), (r3, i3) = g
    sr, si, tr, ti = r0 + r2, i0 + i2, r1 + r3, i1 + i3
    dr, di, er, ei = r0 - r2, i0 - i2, r1 - r3, i1 - i3
    return [(sr + tr, si + ti), (dr - ei, di + er), (sr - tr, si - ti), (dr + ei, di - er)]


def row_kernel(spec, *refs):
    ref = Names(**dict(zip(spec.names, refs)))
    count, rows, quarter = spec.count, spec.rows, spec.quarter
    devs = spec.devs
    per = devs // 4
    step = 16
    total = count * rows
    hi, lo, zs, twiddle = ref.hi, ref.lo, ref.zs, ref.twiddle
    source = spec.source
    if source == "full":
        for j in range(4):
            for q in range(per):
                block = ref.x[per * j + q].reshape(total, lanes)
                high, low = split(block)
                hi[j, :total, q * lanes : (q + 1) * lanes] = high
                lo[j, :total, q * lanes : (q + 1) * lanes] = low
        for j in range(4):
            left = (hi[j, :total, :], lo[j, :total, :])
            zs[j, :total, :] = dot3(left, (ref.inv[0], ref.inv[1]))
    elif source == "band":
        for j in range(4):
            block = ref.x[per * j : per * (j + 1)].reshape(-1, total)
            zs[j, :total, :] = dot3(split(block.T), (ref.inv[0], ref.inv[1]))
    kind = spec.kind
    if kind == "stats":
        stats = [jnp.zeros((8, lanes), f32) for _ in range(spec.stat_rows)]
    if kind == "weigh":
        sums = jnp.sum(ref.stats[...], 0)
        sums = jnp.sum(sums, 1, keepdims=True)
        code = [[ref.code[p, l].astype(f32) for l in range(count)] for p in range(spec.patterns)]
        area = spec.area
        power_mean, count_mean, couple = [], [], []
        base = count + count * (count + 1) // 2
        for p in range(spec.patterns):
            mean = sum(sums[l : l + 1] * code[p][l] for l in range(count)) / area
            mean_count = sums[base + spec.patterns * count + p :][:1] / area
            square = 0.0
            at = count
            for l in range(count):
                for m in range(l, count):
                    factor = 1.0 if l == m else 2.0
                    square = square + (factor * code[p][l] * code[p][m]) * sums[at : at + 1]
                    at += 1
            cross = sum(code[p][l] * sums[base + p * count + l :][:1] for l in range(count))
            power_mean.append(mean)
            count_mean.append(mean_count)
            couple.append((square / mean / mean - cross / mean_count / mean) / area)

    def fold(value):
        total_rows = value[:8]
        for k in range(1, value.shape[0] // 8):
            total_rows = total_rows + value[8 * k : 8 * k + 8]
        out = total_rows[:, :lanes]
        for k in range(1, value.shape[1] // lanes):
            out = out + total_rows[:, lanes * k : lanes * (k + 1)]
        return out

    def chunk(i, carry):
        base_row = pl.multiple_of(i * step, step)
        here = pl.ds(base_row, step)
        fields = []
        for l in range(count):
            at = pl.ds(pl.multiple_of(l * rows + base_row, step), step)
            if source in ("full", "band"):
                parts = [(zs[j, at, :quarter], zs[j, at, quarter:]) for j in range(4)]
                fields.append(row_gather(parts, twiddle))
        cut = [slice(a * quarter, (a + 1) * quarter) for a in range(4)]

        def tilt(l, a, value, sign):
            rc, rs = ref.tilt_r[2 * l, here, :], ref.tilt_r[2 * l + 1, here, :]
            cc, cs = ref.tilt_c[2 * l : 2 * l + 1, cut[a]], ref.tilt_c[2 * l + 1 : 2 * l + 2, cut[a]]
            wide = jnp.concatenate([rc] * (quarter // lanes), 1), jnp.concatenate([rs] * (quarter // lanes), 1)
            er = wide[0] * cc - wide[1] * cs
            ei = sign * (wide[0] * cs + wide[1] * cc)
            re, im = value
            return re * er - im * ei, re * ei + im * er

        outgoing = []
        if kind == "enter":
            outgoing = [[(ref.tr[0, here, c], ref.tr[1, here, c]) for c in cut]]
        elif kind == "forward" or kind == "forward_band":
            for l in range(count):
                at = pl.ds(pl.multiple_of(l * rows + base_row, step), step)
                blocks = []
                for a, c in enumerate(cut):
                    tr, ti = ref.tr[0, here, c], ref.tr[1, here, c]
                    re, im = fields[l][a]
                    re, im = re * tr - im * ti, re * ti + im * tr
                    ref.passed[0, at, c] = re
                    ref.passed[1, at, c] = im
                    blocks.append((re, im) if kind == "forward" else tilt(l, a, (re, im), 1.0))
                outgoing.append(blocks)
        elif kind == "stats":
            adds = [0.0] * spec.stat_rows
            for a, c in enumerate(cut):
                power = []
                for l in range(count):
                    at = pl.ds(pl.multiple_of(l * rows + base_row, step), step)
                    re, im = fields[l][a]
                    ref.passed[0, at, c] = re
                    ref.passed[1, at, c] = im
                    power.append(re * re + im * im)
                values = list(power)
                for l in range(count):
                    for m in range(l, count):
                        values.append(power[l] * power[m])
                seen = [ref.measured[p, here, c].astype(f32) for p in range(spec.patterns)]
                for p in range(spec.patterns):
                    for l in range(count):
                        values.append(seen[p] * power[l])
                values += seen
                for k, value in enumerate(values):
                    adds[k] = adds[k] + fold(value)
            return tuple(x + y for x, y in zip(carry, adds))
        elif kind == "weigh":
            outgoing = [[] for _ in range(count)]
            for a, c in enumerate(cut):
                camera, power = [], []
                for l in range(count):
                    at = pl.ds(pl.multiple_of(l * rows + base_row, step), step)
                    re, im = ref.passed[0, at, c], ref.passed[1, at, c]
                    camera.append((re, im))
                    power.append(re * re + im * im)
                weight = [0.0] * count
                for p in range(spec.patterns):
                    lit = sum(code[p][l] * power[l] for l in range(count))
                    seen = ref.measured[p, here, c].astype(f32)
                    misfit = lit * (1.0 / power_mean[p]) - seen * (1.0 / count_mean[p])
                    pull = (misfit - couple[p]) * (1.0 / power_mean[p])
                    for l in range(count):
                        weight[l] = weight[l] + code[p][l] * pull
                for l in range(count):
                    scale = 2.0 * weight[l]
                    outgoing[l].append((scale * camera[l][0], scale * camera[l][1]))
        elif kind == "back" or kind == "back_band":
            grads = [0.0] * 4
            for l in range(count):
                at = pl.ds(pl.multiple_of(l * rows + base_row, step), step)
                blocks = []
                for a, c in enumerate(cut):
                    re, im = fields[l][a]
                    if kind == "back_band":
                        re, im = tilt(l, a, (re, im), -1.0)
                    pr, pi = ref.passed[0, at, c], ref.passed[1, at, c]
                    grads[a] = grads[a] + (pr * im - pi * re)
                    tr, ti = ref.tr[0, here, c], ref.tr[1, here, c]
                    blocks.append((re * tr + im * ti, im * tr - re * ti))
                outgoing.append(blocks)
            for a, c in enumerate(cut):
                ref.grad[here, c] = grads[a]
        elif kind == "leave":
            for a, c in enumerate(cut):
                tr, ti = ref.tr[0, here, c], ref.tr[1, here, c]
                re, im = fields[0][a]
                ref.grad[here, c] = tr * im - ti * re
        for l, blocks in enumerate(outgoing):
            at = pl.ds(pl.multiple_of(l * rows + base_row, step), step)
            for j, (re, im) in enumerate(row_spread(blocks, twiddle)):
                high, low = split(re)
                hi[j, at, :quarter] = high
                lo[j, at, :quarter] = low
                high, low = split(im)
                hi[j, at, quarter:] = high
                lo[j, at, quarter:] = low
        return carry

    if kind == "stats":
        stats = lax.fori_loop(0, rows // step, chunk, tuple(stats))
        packed = [jnp.sum(row, 0, keepdims=True) for row in stats]
        packed.append(jnp.zeros((ref.sums.shape[1] - len(packed), lanes), f32))
        packed = jnp.concatenate(packed, 0)
        for d in range(devs):
            ref.sums[d] = packed
        return
    lax.fori_loop(0, rows // step, chunk, 0)
    if spec.target == "full":
        for j in range(4):
            y = dot3((hi[j, :total, :], lo[j, :total, :]), (ref.fwd[0], ref.fwd[1]))
            for q in range(per):
                ref.y[per * j + q] = y[:, q * lanes : (q + 1) * lanes].reshape(count, rows, lanes)
    elif spec.target == "band":
        for j in range(4):
            y = dot3((hi[j, :total, :], lo[j, :total, :]), (ref.fwd[0], ref.fwd[1]))
            ref.y[per * j : per * (j + 1)] = y.T.reshape(per, -1, total)


def run_rows(kind, source, target, dims, inputs, outputs):
    spec = Names(**vars(dims), kind=kind, source=source, target=target)
    count = spec.count
    total = count * spec.rows
    wide = 2 * spec.quarter
    names = list(inputs) + list(outputs) + ["hi", "lo", "zs"]
    spec.names = names
    vmem = pl.BlockSpec(memory_space=pltpu.VMEM)
    in_specs = [
        pl.BlockSpec(memory_space=pltpu.SMEM) if name == "code" else vmem for name in inputs
    ]
    return pl.pallas_call(
        functools.partial(row_kernel, spec),
        out_shape=[jax.ShapeDtypeStruct(shape, f32) for shape in outputs.values()],
        in_specs=in_specs,
        out_specs=[vmem] * len(outputs),
        scratch_shapes=[
            pltpu.VMEM((4, total, wide), bf16),
            pltpu.VMEM((4, total, wide), bf16),
            pltpu.VMEM((4, total, wide), f32),
        ],
        name="rows_" + kind,
    )(*inputs.values())


def col_kernel(spec, x_ref, p_ref, w_ref, t_ref, y_ref, hi, lo, zs):
    rows, quarter, devs = spec.rows, spec.quarter, spec.devs
    count_in, count_out, sign = spec.count_in, spec.count_out, spec.sign
    count = p_ref.shape[1]
    per = devs // 4
    weights = (w_ref[0], w_ref[1])

    def spread(i, carry):
        here = pl.ds(pl.multiple_of(i * rows, rows), rows)
        for l in range(count_in):
            x0, x1, x2, x3 = [x_ref[per * a + i, l] for a in range(4)]
            s, t, d, e = x0 + x2, x1 + x3, x0 - x2, turn(x1 - x3)
            for j, value in enumerate((s + t, d + e, s - t, d - e)):
                if j:
                    value = value * t_ref[0, j - 1, here, :] + turn(value) * t_ref[1, j - 1, here, :]
                high, low = split(value)
                hi[j, here, l * lanes : (l + 1) * lanes] = high
                lo[j, here, l * lanes : (l + 1) * lanes] = low
        return carry

    lax.fori_loop(0, per, spread, 0)
    wide_in, wide_out = count_in * lanes, count_out * lanes
    for j in range(4):
        y = dot3(weights, (hi[j, :, :wide_in], lo[j, :, :wide_in]))
        spectra = []
        for l in range(count_in):
            at = slice(l * lanes, (l + 1) * lanes)
            spectra.append(y[:quarter, at] + turn(y[quarter:, at]))
        results = []
        for l in range(count):
            z = spectra[l if count_in > 1 else 0]
            results.append(z * p_ref[0, l, j] - sign * (turn(z) * p_ref[1, l, j]))
        if count_out == 1:
            results = [sum(results)]
        for l in range(count_out):
            high, low = split(results[l])
            hi[j, :, l * lanes : (l + 1) * lanes] = high
            lo[j, :, l * lanes : (l + 1) * lanes] = low
    for j in range(4):
        y = dot3(weights, (hi[j, :, :wide_out], lo[j, :, :wide_out]))
        for l in range(count_out):
            at = slice(l * lanes, (l + 1) * lanes)
            value = y[:quarter, at] - turn(y[quarter:, at])
            if j:
                value = value * t_ref[0, j - 1] - turn(value) * t_ref[1, j - 1]
            zs[j, :, at] = value

    def gather(i, carry):
        here = pl.ds(pl.multiple_of(i * rows, rows), rows)
        for l in range(count_out):
            at = slice(l * lanes, (l + 1) * lanes)
            g0, g1, g2, g3 = [zs[j, here, at] for j in range(4)]
            s, t, d, e = g0 + g2, g1 + g3, g0 - g2, turn(g1 - g3)
            for a, value in enumerate((s + t, d - e, s - t, d + e)):
                y_ref[per * a + i, l] = value
        return carry

    lax.fori_loop(0, per, gather, 0)


def run_cols(x, prop, tables, dims, count_in, count_out, sign):
    spec = Names(**vars(dims), count_in=count_in, count_out=count_out, sign=sign)
    rows, quarter, devs = dims.rows, dims.quarter, dims.devs
    wide = max(count_in, count_out) * lanes
    vmem = pl.BlockSpec(memory_space=pltpu.VMEM)
    return pl.pallas_call(
        functools.partial(col_kernel, spec),
        out_shape=jax.ShapeDtypeStruct((devs, count_out, rows, lanes), f32),
        in_specs=[vmem] * 4,
        out_specs=vmem,
        scratch_shapes=[
            pltpu.VMEM((4, quarter, wide), bf16),
            pltpu.VMEM((4, quarter, wide), bf16),
            pltpu.VMEM((4, quarter, wide), f32),
        ],
        name="cols",
    )(x, prop, jnp.asarray(tables.both), jnp.asarray(tables.twiddle))


def band_kernel(spec, x_ref, p_ref, w_ref, v_ref, y_ref):
    devs, sign, count = spec.devs, spec.sign, spec.count
    half = lanes // 2
    lane = lax.broadcasted_iota(jnp.int32, x_ref.shape[1:], 1)
    pieces = [[], []]
    for s in range(0, devs, 2):
        even, odd = x_ref[s], x_ref[s + 1]
        pieces[0].append(jnp.where(lane < half, even, pltpu.roll(odd, half, 1)))
        pieces[1].append(jnp.where(lane < half, pltpu.roll(even, half, 1), odd))
    field = jnp.concatenate([jnp.concatenate(p, 1) for p in pieces], 0)
    wide = w_ref.shape[2] // 2
    deep = v_ref.shape[2] // 2
    cols = x_ref.shape[1] // 2
    both = dot3(split(field), (w_ref[0], w_ref[1]))
    scaled = []
    for l in range(count):
        re = slice(2 * l * cols, (2 * l + 1) * cols)
        im = slice((2 * l + 1) * cols, (2 * l + 2) * cols)
        yr = both[re, :wide] + both[im, wide:]
        yi = both[im, :wide] - both[re, wide:]
        pr, pi = p_ref[0], sign * p_ref[1]
        scaled += [yr * pr - yi * pi, yr * pi + yi * pr]
    both = dot3(split(jnp.concatenate(scaled, 0)), (v_ref[0], v_ref[1]))
    out = []
    for l in range(count):
        re = slice(2 * l * cols, (2 * l + 1) * cols)
        im = slice((2 * l + 1) * cols, (2 * l + 2) * cols)
        out.append(
            jnp.concatenate(
                [both[re, :deep] - both[im, deep:], both[im, :deep] + both[re, deep:]], 0
            )
        )
    for s in range(0, devs, 2):
        at = slice(s * half, s * half + lanes)
        first, second = out[0][:, at], out[1][:, at]
        y_ref[s] = jnp.where(lane < half, first, pltpu.roll(second, half, 1))
        y_ref[s + 1] = jnp.where(lane < half, pltpu.roll(first, half, 1), second)


def run_band(x, pupil, tables, dims, sign):
    vmem = pl.BlockSpec(memory_space=pltpu.VMEM)
    return pl.pallas_call(
        functools.partial(band_kernel, Names(**vars(dims), sign=sign)),
        out_shape=jax.ShapeDtypeStruct(x.shape, f32),
        in_specs=[vmem] * 4,
        out_specs=vmem,
        name="pupil_cols",
    )(x, pupil, jnp.asarray(tables.band), jnp.asarray(tables.band_inv))


def exchange(x):
    return lax.all_to_all(x, "pat", split_axis=0, concat_axis=0, tiled=True)


def body(slab_phase, pupil_phase, pupil_mask, led_code, led_freq, measured):
    devs = lax.axis_size("pat")
    position = lax.axis_index("pat")
    slab_count, rows, size = slab_phase.shape
    patterns, count = led_code.shape
    quarter, cols, per = size // 4, size // devs, devs // 4
    band = 2 * pupil_radius
    band_cols = band // devs
    dims = Names(
        count=count, rows=rows, quarter=quarter, devs=devs, patterns=patterns,
        area=float(size * size),
    )
    rt = row_tables(size, cols, band_cols)
    ct = col_tables(size)
    shape_full = (devs, count, rows, lanes)
    shape_band = (devs, 2 * band_cols, count * rows)
    shape_field = (2, count * rows, size)
    transmission = [jnp.stack([jnp.cos(slab_phase[s]), jnp.sin(slab_phase[s])]) for s in range(slab_count)]
    twiddle, table = rt.twiddle, rt

    lane = jnp.arange(lanes, dtype=jnp.int32) % cols
    col_index = 4 * ((position % per) * cols + lane) + position // per
    row_index = 4 * jnp.arange(quarter, dtype=jnp.int32)[None, :] + jnp.arange(4, dtype=jnp.int32)[:, None]
    col_freq = frequency(col_index[None, :] + led_freq[:, 1][:, None] + size, size)
    row_freq = frequency(row_index[None] + led_freq[:, 0][:, None, None] + size, size)
    radius = (row_freq * row_freq)[..., None] + (col_freq * col_freq)[:, None, None, :]
    cutoff = size // 2 * (size // 2)
    inside = radius <= cutoff
    height = jnp.sqrt(jnp.maximum(cutoff - radius, 0).astype(f32))
    shift = spread_rate * (height - size // 2)
    prop = jnp.stack([jnp.where(inside, jnp.cos(shift), 0.0), jnp.where(inside, jnp.sin(shift), 0.0)])

    def near(x):
        return jnp.concatenate([x[:, size - pupil_radius :], x[:, :pupil_radius]], 1)

    opening, phase = near(pupil_mask).astype(f32), near(pupil_phase)
    own = jnp.stack([opening * jnp.cos(phase), opening * jnp.sin(phase)])
    own = own.reshape(2, cols // 4, 4, band)
    pupil = 0.0
    owners = [(q - pupil_radius // cols) % devs for q in range(per)]
    for j in range(4):
        pairs = [(owners[q], per * j + q) for q in range(per)]
        pupil = pupil + lax.ppermute(own[:, :, j], "pat", pairs)

    def wave(freq, index):
        turns = (freq[:, None] * index[None, :]) % size
        angle = turns.astype(f32) * (2.0 * math.pi / size)
        return jnp.stack([jnp.cos(angle), jnp.sin(angle)], 1).reshape(2 * count, -1)

    tilt_c = wave(led_freq[:, 1], jnp.arange(size, dtype=jnp.int32))
    tilt_r = wave(led_freq[:, 0], position * rows + jnp.arange(rows, dtype=jnp.int32))
    tilt_r = jnp.broadcast_to(tilt_r[:, :, None], (2 * count, rows, lanes))
    tilts = dict(tilt_r=tilt_r, tilt_c=tilt_c)
    full_both = dict(inv=table.full_inv, fwd=table.full, twiddle=twiddle)

    one = Names(**{**vars(dims), **dict(count=1)})
    (y,) = run_rows(
        "enter", None, "full", one,
        dict(tr=transmission[0], fwd=table.full, twiddle=twiddle),
        dict(y=(devs, 1, rows, lanes)),
    )
    x = exchange(run_cols(exchange(y), prop, ct, dims, 1, count, 1.0))
    y, passed1 = run_rows(
        "forward", "full", "full", dims, dict(x=x, tr=transmission[1], **full_both),
        dict(y=shape_full, passed=shape_field),
    )
    x = exchange(run_cols(exchange(y), prop, ct, dims, count, count, 1.0))
    y, passed2 = run_rows(
        "forward_band", "full", "band", dims,
        dict(x=x, tr=transmission[2], inv=table.full_inv, fwd=table.band, twiddle=twiddle, **tilts),
        dict(y=shape_band, passed=shape_field),
    )
    x = exchange(run_band(exchange(y), pupil, ct, dims, 1.0))
    stat_rows = count + count * (count + 1) // 2 + patterns * count + patterns
    dims.stat_rows = stat_rows
    camera, sums = run_rows(
        "stats", "band", None, dims,
        dict(x=x, inv=table.band_inv, twiddle=twiddle, measured=measured),
        dict(passed=shape_field, sums=(devs, -(-stat_rows // 8) * 8, lanes)),
    )
    (y,) = run_rows(
        "weigh", None, "band", dims,
        dict(stats=exchange(sums), code=led_code, passed=camera, measured=measured, fwd=table.band, twiddle=twiddle),
        dict(y=shape_band),
    )
    x = exchange(run_band(exchange(y), pupil, ct, dims, -1.0))
    y, grad2 = run_rows(
        "back_band", "band", "full", dims,
        dict(x=x, tr=transmission[2], passed=passed2, inv=table.band_inv, fwd=table.full, twiddle=twiddle, **tilts),
        dict(y=shape_full, grad=(rows, size)),
    )
    x = exchange(run_cols(exchange(y), prop, ct, dims, count, count, -1.0))
    y, grad1 = run_rows(
        "back", "full", "full", dims,
        dict(x=x, tr=transmission[1], passed=passed1, **full_both),
        dict(y=shape_full, grad=(rows, size)),
    )
    x = exchange(run_cols(exchange(y), prop, ct, dims, count, 1, -1.0))
    (grad0,) = run_rows(
        "leave", "full", None, one,
        dict(x=x, tr=transmission[0], inv=table.full_inv, twiddle=twiddle),
        dict(grad=(rows, size)),
    )
    return jnp.stack([grad0, grad1, grad2])


def solution(mesh):
    in_specs = (
        P("tiles", "pat", None),
        P("pat", None),
        P("pat", None),
        P(),
        P(),
        P("tiles", "pat", None),
    )
    out_specs = P("tiles", "pat", None)
    def run(slab_phase, *others):
        devs = mesh.shape["pat"]
        size, count = slab_phase.shape[-1], others[2].shape[1]
        fits = 2 * size == lanes * devs and count * size == lanes * devs and slab_phase.shape[0] == 3 * mesh.shape["tiles"]
        inner = body if fits else plain_body
        return jax.shard_map(inner, mesh=mesh, in_specs=in_specs, out_specs=out_specs, check_vma=False)(
            slab_phase, *others
        )

    return run
```

```python
import functools
import math
import types

import jax
import jax.numpy as jnp
import numpy as np
from jax import lax
from jax.experimental import pallas as pl
from jax.experimental.pallas import tpu as pltpu
from jax.sharding import PartitionSpec as P

spread_rate = 0.3
highest = lax.Precision.HIGHEST


def frequency(grid_index, grid_size):
    return (grid_index + grid_size // 2) % grid_size - grid_size // 2


def complex_times(values, factor):
    real_part = values[0] * factor[0] - values[1] * factor[1]
    imag_part = values[0] * factor[1] + values[1] * factor[0]
    return jnp.stack([real_part, imag_part])


def dft_block(length, direction, norm_factor):
    grid_index = jnp.arange(length, dtype=jnp.int32)
    angles = (grid_index[:, None] * grid_index[None, :] % length).astype(jnp.float32) * (
        2.0 * math.pi / length
    )
    cosine = jnp.cos(angles) * norm_factor
    signed_sine = direction * jnp.sin(angles) * norm_factor
    real_rows = jnp.stack([cosine, signed_sine], 1)
    imag_rows = jnp.stack([-signed_sine, cosine], 1)
    return jnp.stack([real_rows, imag_rows], 0)


def twiddle_table(short_size, long_size, grid_size, direction):
    short_index = jnp.arange(short_size, dtype=jnp.int32)
    long_index = jnp.arange(long_size, dtype=jnp.int32)
    angles = (short_index[:, None] * long_index[None, :] % grid_size).astype(jnp.float32) * (
        2.0 * math.pi / grid_size
    )
    return jnp.stack([jnp.cos(angles), direction * jnp.sin(angles)])


def table_set(col_count, dev_count, grid_size, direction):
    short_table = dft_block(col_count, direction, 1.0)
    long_table = dft_block(dev_count, direction, 1.0 / math.sqrt(grid_size))
    return (short_table, long_table, twiddle_table(col_count, dev_count, grid_size, direction))


def to_fourier(wave_field, tables, dev_count):
    short_table, long_table, twiddles = tables
    led_count = wave_field.shape[1]
    row_count = wave_field.shape[2]
    grid_size = wave_field.shape[3]
    col_count = grid_size // dev_count
    shaped = wave_field.reshape(2, led_count, row_count, col_count, dev_count)
    sectioned = jnp.einsum("zlrmq,zmwc->wlrcq", shaped, short_table, precision=highest)
    sectioned = complex_times(sectioned, twiddles)
    outgoing = jnp.einsum("wlrcq,wqvd->dvlcr", sectioned, long_table, precision=highest)
    incoming = lax.all_to_all(
        outgoing.reshape(dev_count, -1), "pat", split_axis=0, concat_axis=0, tiled=True
    )
    incoming = incoming.reshape(dev_count, 2, led_count, col_count, row_count)
    sectioned = jnp.einsum("swlcr,wsvj->vlcrj", incoming, long_table, precision=highest)
    sectioned = complex_times(sectioned, twiddles)
    sectioned = jnp.einsum("wlcrj,wrvh->vlchj", sectioned, short_table, precision=highest)
    return sectioned.reshape(2, led_count, col_count, grid_size)


def to_space(spectrum, tables, dev_count):
    short_table, long_table, twiddles = tables
    led_count = spectrum.shape[1]
    col_count = spectrum.shape[2]
    grid_size = spectrum.shape[3]
    row_count = grid_size // dev_count
    shaped = spectrum.reshape(2, led_count, col_count, row_count, dev_count)
    sectioned = jnp.einsum("zlcmq,zmwr->wlcrq", shaped, short_table, precision=highest)
    sectioned = complex_times(sectioned, twiddles)
    outgoing = jnp.einsum("wlcrq,wqvd->dvlcr", sectioned, long_table, precision=highest)
    incoming = lax.all_to_all(
        outgoing.reshape(dev_count, -1), "pat", split_axis=0, concat_axis=0, tiled=True
    )
    incoming = incoming.reshape(dev_count, 2, led_count, col_count, row_count)
    sectioned = jnp.einsum("swlcr,wsvj->vlrcj", incoming, long_table, precision=highest)
    sectioned = complex_times(sectioned, twiddles)
    sectioned = jnp.einsum("wlrcj,wcvh->vlrhj", sectioned, short_table, precision=highest)
    return sectioned.reshape(2, led_count, row_count, grid_size)


def plain_body(slab_phase, pupil_phase, pupil_mask, led_code, led_freq, measured):
    dev_count = lax.axis_size("pat")
    position = lax.axis_index("pat")
    slab_count, row_count, grid_size = slab_phase.shape
    col_count = grid_size // dev_count
    pattern_count, led_count = led_code.shape
    area = float(grid_size * grid_size)
    forward_set = table_set(col_count, dev_count, grid_size, -1.0)
    inverse_set = table_set(col_count, dev_count, grid_size, 1.0)
    conjugate = jnp.array([1.0, -1.0], jnp.float32)[:, None, None]
    col_freq = frequency(position * col_count + jnp.arange(col_count, dtype=jnp.int32), grid_size)
    row_freq = frequency(jnp.arange(grid_size, dtype=jnp.int32), grid_size)
    radius = col_freq[:, None] * col_freq[:, None] + row_freq[None, :] * row_freq[None, :]
    cutoff = grid_size // 2 * (grid_size // 2)
    inside = radius <= cutoff
    height = jnp.sqrt(jnp.maximum(cutoff - radius, 0).astype(jnp.float32))
    phase_shift = spread_rate * (height - grid_size // 2)
    propagator = jnp.stack(
        [jnp.where(inside, jnp.cos(phase_shift), 0.0), jnp.where(inside, jnp.sin(phase_shift), 0.0)]
    )
    opening = pupil_mask.astype(jnp.float32)
    pupil = jnp.stack([opening * jnp.cos(pupil_phase), opening * jnp.sin(pupil_phase)])
    propagator_conj = propagator * conjugate
    pupil_conj = pupil * conjugate
    row_index = position * row_count + jnp.arange(row_count, dtype=jnp.int32)
    col_index = jnp.arange(grid_size, dtype=jnp.int32)
    tilt_index = (
        led_freq[:, 0][:, None, None] * row_index[None, :, None]
        + led_freq[:, 1][:, None, None] * col_index[None, None, :]
    ) % grid_size
    tilt_angle = tilt_index.astype(jnp.float32) * (2.0 * math.pi / grid_size)
    illumination = jnp.stack([jnp.cos(tilt_angle), jnp.sin(tilt_angle)])
    transmission = jnp.stack([jnp.cos(slab_phase), jnp.sin(slab_phase)])
    group_count = 1
    group_size = led_count // group_count
    wave_groups = [illumination]
    passed_groups = []
    for slab_index in range(slab_count):
        factor = transmission[:, slab_index]
        passed = [complex_times(wave_field, factor) for wave_field in wave_groups]
        passed_groups.append(passed)
        spectral_factor = propagator if slab_index < slab_count - 1 else pupil
        wave_groups = [
            to_space(
                complex_times(to_fourier(passed_field, forward_set, dev_count), spectral_factor),
                inverse_set,
                dev_count,
            )
            for passed_field in passed
        ]
    camera = wave_groups[0]
    led_power = camera[0] * camera[0] + camera[1] * camera[1]
    code_float = led_code.astype(jnp.float32)
    pattern_power = jnp.dot(
        code_float, led_power.reshape(led_count, -1), precision=highest
    ).reshape(pattern_count, row_count, grid_size)
    counts = measured.astype(jnp.float32)
    power_sum, count_sum = lax.psum(
        (jnp.sum(pattern_power, axis=(1, 2)), jnp.sum(counts, axis=(1, 2))), "pat"
    )
    mean_power = power_sum / area
    mean_count = count_sum / area
    relative = pattern_power / mean_power[:, None, None]
    misfit = relative - counts / mean_count[:, None, None]
    coupling = lax.psum(jnp.sum(misfit * relative, axis=(1, 2)), "pat") / area
    pattern_weight = (misfit - coupling[:, None, None]) / mean_power[:, None, None]
    led_weight = jnp.dot(
        code_float.T, pattern_weight.reshape(pattern_count, -1), precision=highest
    ).reshape(led_count, row_count, grid_size)
    camera_adjoint = 2.0 * led_weight[None] * camera
    adjoint_groups = [camera_adjoint]
    gradients = [None] * slab_count
    for slab_index in range(slab_count - 1, -1, -1):
        spectral_factor = pupil_conj if slab_index == slab_count - 1 else propagator_conj
        back_groups = [
            to_space(
                complex_times(to_fourier(adjoint_field, forward_set, dev_count), spectral_factor),
                inverse_set,
                dev_count,
            )
            for adjoint_field in adjoint_groups
        ]
        gradient = jnp.zeros((row_count, grid_size), jnp.float32)
        for passed_field, back_field in zip(passed_groups[slab_index], back_groups):
            gradient = jnp.sum(
                passed_field[0] * back_field[1] - passed_field[1] * back_field[0], axis=0
            )
        gradients[slab_index] = gradient
        if slab_index > 0:
            release = transmission[:, slab_index] * conjugate
            adjoint_groups = [complex_times(back_field, release) for back_field in back_groups]
    return jnp.stack(gradients)


class Names(types.SimpleNamespace):
    pass


pupil_radius = 128
lanes = 128
f32 = jnp.float32
bf16 = jnp.bfloat16


def halves(table):
    table32 = np.asarray(table, np.float32)
    high = table32.astype(bf16)
    low = (table32 - high.astype(np.float32)).astype(bf16)
    return np.stack([high, low])


def row_tables(size, block, band_block):
    quarter = size // 4
    pos = np.arange(quarter)
    angle = 2.0 * np.pi * ((pos[:, None] * pos[None, :]) % quarter) / quarter
    cosine = np.cos(angle) / math.sqrt(size)
    sine = np.sin(angle) / math.sqrt(size)

    def forward(freqs, width):
        parts = []
        for first in range(0, len(freqs), width):
            pick = freqs[first : first + width] % quarter
            left = np.concatenate([cosine[:, pick], sine[:, pick]], 0)
            right = np.concatenate([-sine[:, pick], cosine[:, pick]], 0)
            parts.append(np.concatenate([left, right], 1))
        return np.concatenate(parts, 1)

    full = forward(pos, block)
    reach = pupil_radius // 4
    band = forward(np.arange(-reach, reach), band_block)
    theta = 2.0 * np.pi * (np.arange(4)[:, None] * pos[None, :]) / size
    twiddle = np.concatenate([np.cos(theta), np.sin(theta)], 0).astype(np.float32)
    return Names(
        full=jnp.asarray(halves(full)),
        full_inv=jnp.asarray(halves(full.T)),
        band=jnp.asarray(halves(band)),
        band_inv=jnp.asarray(halves(band.T)),
        twiddle=jnp.asarray(twiddle),
    )


def col_tables(size):
    quarter = size // 4
    pos = np.arange(quarter)
    angle = 2.0 * np.pi * ((pos[:, None] * pos[None, :]) % quarter) / quarter
    both = np.concatenate([np.cos(angle), np.sin(angle)], 0) / math.sqrt(size)
    theta = 2.0 * np.pi * (np.arange(1, 4)[:, None] * pos[None, :]) / size
    twiddle = np.stack([np.cos(theta), np.sin(theta)]).astype(np.float32)
    twiddle = np.ascontiguousarray(np.broadcast_to(twiddle[..., None], twiddle.shape + (lanes,)))
    freqs = np.arange(-pupil_radius, pupil_radius)
    angle = 2.0 * np.pi * ((np.arange(size)[:, None] * freqs[None, :]) % size) / size
    cosine = np.cos(angle) / math.sqrt(size)
    sine = np.sin(angle) / math.sqrt(size)
    band = halves(np.concatenate([cosine, sine], 1))
    band_inv = halves(np.concatenate([cosine.T, sine.T], 1))
    return Names(both=halves(both), twiddle=twiddle, band=band, band_inv=band_inv)


def split(value):
    high = value.astype(bf16)
    return high, (value - high.astype(f32)).astype(bf16)


def dot3(left, right):
    def dot(a, b):
        return jnp.dot(a, b, preferred_element_type=f32)

    return dot(left[0], right[0]) + (dot(left[0], right[1]) + dot(left[1], right[0]))


def turn(value):
    rolled = pltpu.roll(value, lanes // 2, 1)
    lane = lax.broadcasted_iota(jnp.int32, value.shape, 1)
    return jnp.where(lane < lanes // 2, rolled, -rolled)


def partner(me, step, devs):
    return lax.rem(me + step, devs)


def greet(devs):
    me = lax.axis_index("pat")
    barrier = pltpu.get_barrier_semaphore()

    def signal(step, carry):
        pl.semaphore_signal(
            barrier, inc=1, device_id=dict(pat=partner(me, step, devs)),
            device_id_type=pl.DeviceIdType.MESH,
        )
        return carry

    lax.fori_loop(1, devs, signal, 0)
    return me, barrier


def remote(ref, me, dest):
    block = ref.stage if ref.same else ref.stage.at[dest]
    return pltpu.make_async_remote_copy(
        src_ref=block, dst_ref=ref.y.at[me], send_sem=ref.sent.at[dest],
        recv_sem=ref.got.at[me], device_id=dict(pat=dest), device_id_type=pl.DeviceIdType.MESH,
    )


def send(ref, me, dest):
    @pl.when(dest != me)
    def _():
        remote(ref, me, dest).start()

    @pl.when(dest == me)
    def _():
        keep(ref, me).start()


def keep(ref, me):
    block = ref.stage if ref.same else ref.stage.at[me]
    return pltpu.make_async_copy(block, ref.y.at[me], ref.kept)


def finish(ref, me, devs):
    def settle(step, carry):
        other = partner(me, step, devs)
        block = ref.stage if ref.same else ref.stage.at[other]
        pltpu.make_async_remote_copy(
            src_ref=block, dst_ref=ref.y.at[other], send_sem=ref.sent.at[other],
            recv_sem=ref.got.at[other], device_id=dict(pat=other),
            device_id_type=pl.DeviceIdType.MESH,
        ).wait()
        return carry

    keep(ref, me).wait()
    lax.fori_loop(1, devs, settle, 0)


def comm_scratch(stage_shape, devs):
    return [
        pltpu.VMEM(stage_shape, f32),
        pltpu.SemaphoreType.DMA((devs,)),
        pltpu.SemaphoreType.DMA((devs,)),
        pltpu.SemaphoreType.DMA,
    ]


def comm_params(channel):
    return pltpu.CompilerParams(collective_id=channel, has_side_effects=True)


anywhere = pl.BlockSpec(memory_space=pl.ANY)


def row_spread(blocks, twiddle_ref):
    (r0, i0), (r1, i1), (r2, i2), (r3, i3) = blocks
    sr, si, tr, ti = r0 + r2, i0 + i2, r1 + r3, i1 + i3
    dr, di, er, ei = r0 - r2, i0 - i2, r1 - r3, i1 - i3
    mixed = [(sr + tr, si + ti), (dr + ei, di - er), (sr - tr, si - ti), (dr - ei, di + er)]
    out = [mixed[0]]
    for j in range(1, 4):
        cosine, sine = twiddle_ref[j : j + 1, :], twiddle_ref[4 + j : 5 + j, :]
        re, im = mixed[j]
        out.append((re * cosine + im * sine, im * cosine - re * sine))
    return out


def row_gather(parts, twiddle_ref):
    g = [parts[0]]
    for j in range(1, 4):
        cosine, sine = twiddle_ref[j : j + 1, :], twiddle_ref[4 + j : 5 + j, :]
        re, im = parts[j]
        g.append((re * cosine - im * sine, im * cosine + re * sine))
    (r0, i0), (r1, i1), (r2, i2), (r3, i3) = g
    sr, si, tr, ti = r0 + r2, i0 + i2, r1 + r3, i1 + i3
    dr, di, er, ei = r0 - r2, i0 - i2, r1 - r3, i1 - i3
    return [(sr + tr, si + ti), (dr - ei, di + er), (sr - tr, si - ti), (dr + ei, di - er)]


def row_kernel(spec, *refs):
    ref = Names(**dict(zip(spec.names, refs)), same=spec.kind == "stats")
    sends = spec.kind != "leave"
    if sends:
        me, barrier = greet(spec.devs)
    count, rows, quarter = spec.count, spec.rows, spec.quarter
    devs = spec.devs
    per = devs // 4
    step = 16
    total = count * rows
    hi, lo, zs, twiddle = ref.hi, ref.lo, ref.zs, ref.twiddle
    source = spec.source
    if source == "full":
        for j in range(4):
            for q in range(per):
                block = ref.x[per * j + q].reshape(total, lanes)
                high, low = split(block)
                hi[j, :total, q * lanes : (q + 1) * lanes] = high
                lo[j, :total, q * lanes : (q + 1) * lanes] = low
        for j in range(4):
            left = (hi[j, :total, :], lo[j, :total, :])
            zs[j, :total, :] = dot3(left, (ref.inv[0], ref.inv[1]))
    elif source == "band":
        for j in range(4):
            block = ref.x[per * j : per * (j + 1)].reshape(-1, total)
            zs[j, :total, :] = dot3(split(block.T), (ref.inv[0], ref.inv[1]))
    kind = spec.kind
    if kind == "stats":
        stats = [jnp.zeros((8, lanes), f32) for _ in range(spec.stat_rows)]
    if kind == "weigh":
        sums = jnp.sum(ref.stats[...], 0)
        sums = jnp.sum(sums, 1, keepdims=True)
        code = [[ref.code[p, l].astype(f32) for l in range(count)] for p in range(spec.patterns)]
        area = spec.area
        power_mean, count_mean, couple = [], [], []
        base = count + count * (count + 1) // 2
        for p in range(spec.patterns):
            mean = sum(sums[l : l + 1] * code[p][l] for l in range(count)) / area
            mean_count = sums[base + spec.patterns * count + p :][:1] / area
            square = 0.0
            at = count
            for l in range(count):
                for m in range(l, count):
                    factor = 1.0 if l == m else 2.0
                    square = square + (factor * code[p][l] * code[p][m]) * sums[at : at + 1]
                    at += 1
            cross = sum(code[p][l] * sums[base + p * count + l :][:1] for l in range(count))
            power_mean.append(mean)
            count_mean.append(mean_count)
            couple.append((square / mean / mean - cross / mean_count / mean) / area)

    def fold(value):
        total_rows = value[:8]
        for k in range(1, value.shape[0] // 8):
            total_rows = total_rows + value[8 * k : 8 * k + 8]
        out = total_rows[:, :lanes]
        for k in range(1, value.shape[1] // lanes):
            out = out + total_rows[:, lanes * k : lanes * (k + 1)]
        return out

    def chunk(i, carry):
        base_row = pl.multiple_of(i * step, step)
        here = pl.ds(base_row, step)
        fields = []
        for l in range(count):
            at = pl.ds(pl.multiple_of(l * rows + base_row, step), step)
            if source in ("full", "band"):
                parts = [(zs[j, at, :quarter], zs[j, at, quarter:]) for j in range(4)]
                fields.append(row_gather(parts, twiddle))
        cut = [slice(a * quarter, (a + 1) * quarter) for a in range(4)]

        def tilt(l, a, value, sign):
            rc, rs = ref.tilt_r[2 * l, here, :], ref.tilt_r[2 * l + 1, here, :]
            cc, cs = ref.tilt_c[2 * l : 2 * l + 1, cut[a]], ref.tilt_c[2 * l + 1 : 2 * l + 2, cut[a]]
            wide = jnp.concatenate([rc] * (quarter // lanes), 1), jnp.concatenate([rs] * (quarter // lanes), 1)
            er = wide[0] * cc - wide[1] * cs
            ei = sign * (wide[0] * cs + wide[1] * cc)
            re, im = value
            return re * er - im * ei, re * ei + im * er

        outgoing = []
        if kind == "enter":
            outgoing = [[(ref.tr[0, here, c], ref.tr[1, here, c]) for c in cut]]
        elif kind == "forward" or kind == "forward_band":
            for l in range(count):
                at = pl.ds(pl.multiple_of(l * rows + base_row, step), step)
                blocks = []
                for a, c in enumerate(cut):
                    tr, ti = ref.tr[0, here, c], ref.tr[1, here, c]
                    re, im = fields[l][a]
                    re, im = re * tr - im * ti, re * ti + im * tr
                    ref.passed[0, at, c] = re
                    ref.passed[1, at, c] = im
                    blocks.append((re, im) if kind == "forward" else tilt(l, a, (re, im), 1.0))
                outgoing.append(blocks)
        elif kind == "stats":
            adds = [0.0] * spec.stat_rows
            for a, c in enumerate(cut):
                power = []
                for l in range(count):
                    at = pl.ds(pl.multiple_of(l * rows + base_row, step), step)
                    re, im = fields[l][a]
                    ref.passed[0, at, c] = re
                    ref.passed[1, at, c] = im
                    power.append(re * re + im * im)
                values = list(power)
                for l in range(count):
                    for m in range(l, count):
                        values.append(power[l] * power[m])
                seen = [ref.measured[p, here, c].astype(f32) for p in range(spec.patterns)]
                for p in range(spec.patterns):
                    for l in range(count):
                        values.append(seen[p] * power[l])
                values += seen
                for k, value in enumerate(values):
                    adds[k] = adds[k] + fold(value)
            return tuple(x + y for x, y in zip(carry, adds))
        elif kind == "weigh":
            outgoing = [[] for _ in range(count)]
            for a, c in enumerate(cut):
                camera, power = [], []
                for l in range(count):
                    at = pl.ds(pl.multiple_of(l * rows + base_row, step), step)
                    re, im = ref.passed[0, at, c], ref.passed[1, at, c]
                    camera.append((re, im))
                    power.append(re * re + im * im)
                weight = [0.0] * count
                for p in range(spec.patterns):
                    lit = sum(code[p][l] * power[l] for l in range(count))
                    seen = ref.measured[p, here, c].astype(f32)
                    misfit = lit * (1.0 / power_mean[p]) - seen * (1.0 / count_mean[p])
                    pull = (misfit - couple[p]) * (1.0 / power_mean[p])
                    for l in range(count):
                        weight[l] = weight[l] + code[p][l] * pull
                for l in range(count):
                    scale = 2.0 * weight[l]
                    outgoing[l].append((scale * camera[l][0], scale * camera[l][1]))
        elif kind == "back" or kind == "back_band":
            grads = [0.0] * 4
            for l in range(count):
                at = pl.ds(pl.multiple_of(l * rows + base_row, step), step)
                blocks = []
                for a, c in enumerate(cut):
                    re, im = fields[l][a]
                    if kind == "back_band":
                        re, im = tilt(l, a, (re, im), -1.0)
                    pr, pi = ref.passed[0, at, c], ref.passed[1, at, c]
                    grads[a] = grads[a] + (pr * im - pi * re)
                    tr, ti = ref.tr[0, here, c], ref.tr[1, here, c]
                    blocks.append((re * tr + im * ti, im * tr - re * ti))
                outgoing.append(blocks)
            for a, c in enumerate(cut):
                ref.grad[here, c] = grads[a]
        elif kind == "leave":
            for a, c in enumerate(cut):
                tr, ti = ref.tr[0, here, c], ref.tr[1, here, c]
                re, im = fields[0][a]
                ref.grad[here, c] = tr * im - ti * re
        for l, blocks in enumerate(outgoing):
            at = pl.ds(pl.multiple_of(l * rows + base_row, step), step)
            for j, (re, im) in enumerate(row_spread(blocks, twiddle)):
                high, low = split(re)
                hi[j, at, :quarter] = high
                lo[j, at, :quarter] = low
                high, low = split(im)
                hi[j, at, quarter:] = high
                lo[j, at, quarter:] = low
        return carry

    if kind == "stats":
        stats = lax.fori_loop(0, rows // step, chunk, tuple(stats))
        packed = [jnp.sum(row, 0, keepdims=True) for row in stats]
        packed.append(jnp.zeros((ref.stage.shape[0] - len(packed), lanes), f32))
        packed = jnp.concatenate(packed, 0)
        ref.stage[...] = packed
        pl.semaphore_wait(barrier, devs - 1)

        def share(k, carry):
            send(ref, me, partner(me, k, devs))
            return carry

        lax.fori_loop(0, devs, share, 0)
        finish(ref, me, devs)
        return
    lax.fori_loop(0, rows // step, chunk, 0)
    if not sends:
        return
    pl.semaphore_wait(barrier, devs - 1)

    def emit(step_j, carry):
        j = lax.rem(me // per + step_j, 4)
        y = dot3((hi[j, :total, :], lo[j, :total, :]), (ref.fwd[0], ref.fwd[1]))
        if spec.target == "full":
            for q in range(per):
                ref.stage[per * j + q] = y[:, q * lanes : (q + 1) * lanes].reshape(count, rows, lanes)
        else:
            flipped = y.T
            deep = flipped.shape[0] // per
            for q in range(per):
                ref.stage[per * j + q] = flipped[q * deep : (q + 1) * deep]
        for q in range(per):
            send(ref, me, per * j + lax.rem(me + q, per))
        return carry

    lax.fori_loop(0, 4, emit, 0)
    finish(ref, me, devs)


def run_rows(channel, kind, source, target, dims, inputs, outputs):
    spec = Names(**vars(dims), kind=kind, source=source, target=target)
    count = spec.count
    total = count * spec.rows
    wide = 2 * spec.quarter
    names = list(inputs) + list(outputs) + ["hi", "lo", "zs"]
    sends = "y" in outputs
    comm = []
    if sends:
        names += ["stage", "sent", "got", "kept"]
        shape = outputs["y"]
        comm = comm_scratch(shape[1:] if kind == "stats" else shape, spec.devs)
    spec.names = names
    vmem = pl.BlockSpec(memory_space=pltpu.VMEM)
    in_specs = [
        pl.BlockSpec(memory_space=pltpu.SMEM) if name == "code" else vmem for name in inputs
    ]
    return pl.pallas_call(
        functools.partial(row_kernel, spec),
        out_shape=[jax.ShapeDtypeStruct(shape, f32) for shape in outputs.values()],
        in_specs=in_specs,
        out_specs=[anywhere if name == "y" else vmem for name in outputs],
        scratch_shapes=[
            pltpu.VMEM((4, total, wide), bf16),
            pltpu.VMEM((4, total, wide), bf16),
            pltpu.VMEM((4, total, wide), f32),
        ]
        + comm,
        compiler_params=comm_params(channel) if sends else None,
        name="rows_" + kind,
    )(*inputs.values())


def col_kernel(spec, x_ref, p_ref, w_ref, t_ref, y_ref, hi, lo, zs, stage, sent, got, kept):
    ref = Names(y=y_ref, stage=stage, sent=sent, got=got, kept=kept, same=False)
    me, barrier = greet(spec.devs)
    rows, quarter, devs = spec.rows, spec.quarter, spec.devs
    count_in, count_out, sign = spec.count_in, spec.count_out, spec.sign
    count = p_ref.shape[1]
    per = devs // 4
    weights = (w_ref[0], w_ref[1])

    def spread(i, carry):
        here = pl.ds(pl.multiple_of(i * rows, rows), rows)
        for l in range(count_in):
            x0, x1, x2, x3 = [x_ref[per * a + i, l] for a in range(4)]
            s, t, d, e = x0 + x2, x1 + x3, x0 - x2, turn(x1 - x3)
            for j, value in enumerate((s + t, d + e, s - t, d - e)):
                if j:
                    value = value * t_ref[0, j - 1, here, :] + turn(value) * t_ref[1, j - 1, here, :]
                high, low = split(value)
                hi[j, here, l * lanes : (l + 1) * lanes] = high
                lo[j, here, l * lanes : (l + 1) * lanes] = low
        return carry

    lax.fori_loop(0, per, spread, 0)
    wide_in, wide_out = count_in * lanes, count_out * lanes
    for j in range(4):
        y = dot3(weights, (hi[j, :, :wide_in], lo[j, :, :wide_in]))
        spectra = []
        for l in range(count_in):
            at = slice(l * lanes, (l + 1) * lanes)
            spectra.append(y[:quarter, at] + turn(y[quarter:, at]))
        results = []
        for l in range(count):
            z = spectra[l if count_in > 1 else 0]
            results.append(z * p_ref[0, l, j] - sign * (turn(z) * p_ref[1, l, j]))
        if count_out == 1:
            results = [sum(results)]
        for l in range(count_out):
            high, low = split(results[l])
            hi[j, :, l * lanes : (l + 1) * lanes] = high
            lo[j, :, l * lanes : (l + 1) * lanes] = low
    for j in range(4):
        y = dot3(weights, (hi[j, :, :wide_out], lo[j, :, :wide_out]))
        for l in range(count_out):
            at = slice(l * lanes, (l + 1) * lanes)
            value = y[:quarter, at] - turn(y[quarter:, at])
            if j:
                value = value * t_ref[0, j - 1] - turn(value) * t_ref[1, j - 1]
            zs[j, :, at] = value

    pl.semaphore_wait(barrier, devs - 1)

    def gather(step, carry):
        i = lax.rem(me + step, per)
        here = pl.ds(pl.multiple_of(i * rows, rows), rows)
        for l in range(count_out):
            at = slice(l * lanes, (l + 1) * lanes)
            g0, g1, g2, g3 = [zs[j, here, at] for j in range(4)]
            s, t, d, e = g0 + g2, g1 + g3, g0 - g2, turn(g1 - g3)
            for a, value in enumerate((s + t, d - e, s - t, d + e)):
                stage[per * a + i, l] = value
        for a in range(4):
            send(ref, me, lax.rem(me // per + a, 4) * per + i)
        return carry

    lax.fori_loop(0, per, gather, 0)
    finish(ref, me, devs)


def run_cols(channel, x, prop, tables, dims, count_in, count_out, sign):
    spec = Names(**vars(dims), count_in=count_in, count_out=count_out, sign=sign)
    rows, quarter, devs = dims.rows, dims.quarter, dims.devs
    wide = max(count_in, count_out) * lanes
    vmem = pl.BlockSpec(memory_space=pltpu.VMEM)
    return pl.pallas_call(
        functools.partial(col_kernel, spec),
        out_shape=jax.ShapeDtypeStruct((devs, count_out, rows, lanes), f32),
        in_specs=[vmem] * 4,
        out_specs=anywhere,
        scratch_shapes=[
            pltpu.VMEM((4, quarter, wide), bf16),
            pltpu.VMEM((4, quarter, wide), bf16),
            pltpu.VMEM((4, quarter, wide), f32),
        ]
        + comm_scratch((devs, count_out, rows, lanes), devs),
        compiler_params=comm_params(channel),
        name="cols",
    )(x, prop, jnp.asarray(tables.both), jnp.asarray(tables.twiddle))


def band_kernel(spec, x_ref, p_ref, w_ref, v_ref, y_ref, stage, sent, got, kept):
    ref = Names(y=y_ref, stage=stage, sent=sent, got=got, kept=kept, same=False)
    me, barrier = greet(spec.devs)
    devs, sign, count = spec.devs, spec.sign, spec.count
    half = lanes // 2
    lane = lax.broadcasted_iota(jnp.int32, x_ref.shape[1:], 1)
    pieces = [[], []]
    for s in range(0, devs, 2):
        even, odd = x_ref[s], x_ref[s + 1]
        pieces[0].append(jnp.where(lane < half, even, pltpu.roll(odd, half, 1)))
        pieces[1].append(jnp.where(lane < half, pltpu.roll(even, half, 1), odd))
    field = jnp.concatenate([jnp.concatenate(p, 1) for p in pieces], 0)
    wide = w_ref.shape[2] // 2
    deep = v_ref.shape[2] // 2
    cols = x_ref.shape[1] // 2
    both = dot3(split(field), (w_ref[0], w_ref[1]))
    scaled = []
    for l in range(count):
        re = slice(2 * l * cols, (2 * l + 1) * cols)
        im = slice((2 * l + 1) * cols, (2 * l + 2) * cols)
        yr = both[re, :wide] + both[im, wide:]
        yi = both[im, :wide] - both[re, wide:]
        pr, pi = p_ref[0], sign * p_ref[1]
        scaled += [yr * pr - yi * pi, yr * pi + yi * pr]
    both = dot3(split(jnp.concatenate(scaled, 0)), (v_ref[0], v_ref[1]))
    out = []
    for l in range(count):
        re = slice(2 * l * cols, (2 * l + 1) * cols)
        im = slice((2 * l + 1) * cols, (2 * l + 2) * cols)
        out.append(
            jnp.concatenate(
                [both[re, :deep] - both[im, deep:], both[im, :deep] + both[re, deep:]], 0
            )
        )
    for s in range(0, devs, 2):
        at = slice(s * half, s * half + lanes)
        first, second = out[0][:, at], out[1][:, at]
        stage[s] = jnp.where(lane < half, first, pltpu.roll(second, half, 1))
        stage[s + 1] = jnp.where(lane < half, pltpu.roll(first, half, 1), second)
    pl.semaphore_wait(barrier, devs - 1)

    def share(k, carry):
        send(ref, me, partner(me, k, devs))
        return carry

    lax.fori_loop(0, devs, share, 0)
    finish(ref, me, devs)


def run_band(channel, x, pupil, tables, dims, sign):
    vmem = pl.BlockSpec(memory_space=pltpu.VMEM)
    return pl.pallas_call(
        functools.partial(band_kernel, Names(**vars(dims), sign=sign)),
        out_shape=jax.ShapeDtypeStruct(x.shape, f32),
        in_specs=[vmem] * 4,
        out_specs=anywhere,
        scratch_shapes=comm_scratch(x.shape, dims.devs),
        compiler_params=comm_params(channel),
        name="pupil_cols",
    )(x, pupil, jnp.asarray(tables.band), jnp.asarray(tables.band_inv))


def body(slab_phase, pupil_phase, pupil_mask, led_code, led_freq, measured):
    devs = lax.axis_size("pat")
    position = lax.axis_index("pat")
    slab_count, rows, size = slab_phase.shape
    patterns, count = led_code.shape
    quarter, cols, per = size // 4, size // devs, devs // 4
    band = 2 * pupil_radius
    band_cols = band // devs
    dims = Names(
        count=count, rows=rows, quarter=quarter, devs=devs, patterns=patterns,
        area=float(size * size),
    )
    rt = row_tables(size, cols, band_cols)
    ct = col_tables(size)
    shape_full = (devs, count, rows, lanes)
    shape_band = (devs, 2 * band_cols, count * rows)
    shape_field = (2, count * rows, size)
    transmission = [jnp.stack([jnp.cos(slab_phase[s]), jnp.sin(slab_phase[s])]) for s in range(slab_count)]
    twiddle, table = rt.twiddle, rt

    lane = jnp.arange(lanes, dtype=jnp.int32) % cols
    col_index = 4 * ((position % per) * cols + lane) + position // per
    row_index = 4 * jnp.arange(quarter, dtype=jnp.int32)[None, :] + jnp.arange(4, dtype=jnp.int32)[:, None]
    col_freq = frequency(col_index[None, :] + led_freq[:, 1][:, None] + size, size)
    row_freq = frequency(row_index[None] + led_freq[:, 0][:, None, None] + size, size)
    radius = (row_freq * row_freq)[..., None] + (col_freq * col_freq)[:, None, None, :]
    cutoff = size // 2 * (size // 2)
    inside = radius <= cutoff
    height = jnp.sqrt(jnp.maximum(cutoff - radius, 0).astype(f32))
    shift = spread_rate * (height - size // 2)
    prop = jnp.stack([jnp.where(inside, jnp.cos(shift), 0.0), jnp.where(inside, jnp.sin(shift), 0.0)])

    def near(x):
        return jnp.concatenate([x[:, size - pupil_radius :], x[:, :pupil_radius]], 1)

    opening, phase = near(pupil_mask).astype(f32), near(pupil_phase)
    own = jnp.stack([opening * jnp.cos(phase), opening * jnp.sin(phase)])
    own = own.reshape(2, cols // 4, 4, band)
    pupil = 0.0
    owners = [(q - pupil_radius // cols) % devs for q in range(per)]
    for j in range(4):
        pairs = [(owners[q], per * j + q) for q in range(per)]
        pupil = pupil + lax.ppermute(own[:, :, j], "pat", pairs)

    def wave(freq, index):
        turns = (freq[:, None] * index[None, :]) % size
        angle = turns.astype(f32) * (2.0 * math.pi / size)
        return jnp.stack([jnp.cos(angle), jnp.sin(angle)], 1).reshape(2 * count, -1)

    tilt_c = wave(led_freq[:, 1], jnp.arange(size, dtype=jnp.int32))
    tilt_r = wave(led_freq[:, 0], position * rows + jnp.arange(rows, dtype=jnp.int32))
    tilt_r = jnp.broadcast_to(tilt_r[:, :, None], (2 * count, rows, lanes))
    tilts = dict(tilt_r=tilt_r, tilt_c=tilt_c)
    full_both = dict(inv=table.full_inv, fwd=table.full, twiddle=twiddle)

    one = Names(**{**vars(dims), **dict(count=1)})
    (y,) = run_rows(
        7, "enter", None, "full", one,
        dict(tr=transmission[0], fwd=table.full, twiddle=twiddle),
        dict(y=(devs, 1, rows, lanes)),
    )
    x = run_cols(1, y, prop, ct, dims, 1, count, 1.0)
    y, passed1 = run_rows(
        8, "forward", "full", "full", dims, dict(x=x, tr=transmission[1], **full_both),
        dict(y=shape_full, passed=shape_field),
    )
    x = run_cols(2, y, prop, ct, dims, count, count, 1.0)
    y, passed2 = run_rows(
        9, "forward_band", "full", "band", dims,
        dict(x=x, tr=transmission[2], inv=table.full_inv, fwd=table.band, twiddle=twiddle, **tilts),
        dict(y=shape_band, passed=shape_field),
    )
    x = run_band(3, y, pupil, ct, dims, 1.0)
    stat_rows = count + count * (count + 1) // 2 + patterns * count + patterns
    dims.stat_rows = stat_rows
    camera, sums = run_rows(
        10, "stats", "band", None, dims,
        dict(x=x, inv=table.band_inv, twiddle=twiddle, measured=measured),
        dict(passed=shape_field, y=(devs, -(-stat_rows // 8) * 8, lanes)),
    )
    (y,) = run_rows(
        11, "weigh", None, "band", dims,
        dict(stats=sums, code=led_code, passed=camera, measured=measured, fwd=table.band, twiddle=twiddle),
        dict(y=shape_band),
    )
    x = run_band(4, y, pupil, ct, dims, -1.0)
    y, grad2 = run_rows(
        12, "back_band", "band", "full", dims,
        dict(x=x, tr=transmission[2], passed=passed2, inv=table.band_inv, fwd=table.full, twiddle=twiddle, **tilts),
        dict(y=shape_full, grad=(rows, size)),
    )
    x = run_cols(5, y, prop, ct, dims, count, count, -1.0)
    y, grad1 = run_rows(
        13, "back", "full", "full", dims,
        dict(x=x, tr=transmission[1], passed=passed1, **full_both),
        dict(y=shape_full, grad=(rows, size)),
    )
    x = run_cols(6, y, prop, ct, dims, count, 1, -1.0)
    (grad0,) = run_rows(
        14, "leave", "full", None, one,
        dict(x=x, tr=transmission[0], inv=table.full_inv, twiddle=twiddle),
        dict(grad=(rows, size)),
    )
    return jnp.stack([grad0, grad1, grad2])


def solution(mesh):
    in_specs = (
        P("tiles", "pat", None),
        P("pat", None),
        P("pat", None),
        P(),
        P(),
        P("tiles", "pat", None),
    )
    out_specs = P("tiles", "pat", None)
    def run(slab_phase, *others):
        devs = mesh.shape["pat"]
        size, count = slab_phase.shape[-1], others[2].shape[1]
        fits = 2 * size == lanes * devs and count * size == lanes * devs and slab_phase.shape[0] == 3 * mesh.shape["tiles"]
        inner = body if fits else plain_body
        return jax.shard_map(inner, mesh=mesh, in_specs=in_specs, out_specs=out_specs, check_vma=False)(
            slab_phase, *others
        )

    return run
```

```python
import functools
import math
import types

import jax
import jax.numpy as jnp
import numpy as np
from jax import lax
from jax.experimental import pallas as pl
from jax.experimental.pallas import tpu as pltpu
from jax.sharding import PartitionSpec as P

spread_rate = 0.3
highest = lax.Precision.HIGHEST


def frequency(grid_index, grid_size):
    return (grid_index + grid_size // 2) % grid_size - grid_size // 2


def complex_times(values, factor):
    real_part = values[0] * factor[0] - values[1] * factor[1]
    imag_part = values[0] * factor[1] + values[1] * factor[0]
    return jnp.stack([real_part, imag_part])


def dft_block(length, direction, norm_factor):
    grid_index = jnp.arange(length, dtype=jnp.int32)
    angles = (grid_index[:, None] * grid_index[None, :] % length).astype(jnp.float32) * (
        2.0 * math.pi / length
    )
    cosine = jnp.cos(angles) * norm_factor
    signed_sine = direction * jnp.sin(angles) * norm_factor
    real_rows = jnp.stack([cosine, signed_sine], 1)
    imag_rows = jnp.stack([-signed_sine, cosine], 1)
    return jnp.stack([real_rows, imag_rows], 0)


def twiddle_table(short_size, long_size, grid_size, direction):
    short_index = jnp.arange(short_size, dtype=jnp.int32)
    long_index = jnp.arange(long_size, dtype=jnp.int32)
    angles = (short_index[:, None] * long_index[None, :] % grid_size).astype(jnp.float32) * (
        2.0 * math.pi / grid_size
    )
    return jnp.stack([jnp.cos(angles), direction * jnp.sin(angles)])


def table_set(col_count, dev_count, grid_size, direction):
    short_table = dft_block(col_count, direction, 1.0)
    long_table = dft_block(dev_count, direction, 1.0 / math.sqrt(grid_size))
    return (short_table, long_table, twiddle_table(col_count, dev_count, grid_size, direction))


def to_fourier(wave_field, tables, dev_count):
    short_table, long_table, twiddles = tables
    led_count = wave_field.shape[1]
    row_count = wave_field.shape[2]
    grid_size = wave_field.shape[3]
    col_count = grid_size // dev_count
    shaped = wave_field.reshape(2, led_count, row_count, col_count, dev_count)
    sectioned = jnp.einsum("zlrmq,zmwc->wlrcq", shaped, short_table, precision=highest)
    sectioned = complex_times(sectioned, twiddles)
    outgoing = jnp.einsum("wlrcq,wqvd->dvlcr", sectioned, long_table, precision=highest)
    incoming = lax.all_to_all(
        outgoing.reshape(dev_count, -1), "pat", split_axis=0, concat_axis=0, tiled=True
    )
    incoming = incoming.reshape(dev_count, 2, led_count, col_count, row_count)
    sectioned = jnp.einsum("swlcr,wsvj->vlcrj", incoming, long_table, precision=highest)
    sectioned = complex_times(sectioned, twiddles)
    sectioned = jnp.einsum("wlcrj,wrvh->vlchj", sectioned, short_table, precision=highest)
    return sectioned.reshape(2, led_count, col_count, grid_size)


def to_space(spectrum, tables, dev_count):
    short_table, long_table, twiddles = tables
    led_count = spectrum.shape[1]
    col_count = spectrum.shape[2]
    grid_size = spectrum.shape[3]
    row_count = grid_size // dev_count
    shaped = spectrum.reshape(2, led_count, col_count, row_count, dev_count)
    sectioned = jnp.einsum("zlcmq,zmwr->wlcrq", shaped, short_table, precision=highest)
    sectioned = complex_times(sectioned, twiddles)
    outgoing = jnp.einsum("wlcrq,wqvd->dvlcr", sectioned, long_table, precision=highest)
    incoming = lax.all_to_all(
        outgoing.reshape(dev_count, -1), "pat", split_axis=0, concat_axis=0, tiled=True
    )
    incoming = incoming.reshape(dev_count, 2, led_count, col_count, row_count)
    sectioned = jnp.einsum("swlcr,wsvj->vlrcj", incoming, long_table, precision=highest)
    sectioned = complex_times(sectioned, twiddles)
    sectioned = jnp.einsum("wlrcj,wcvh->vlrhj", sectioned, short_table, precision=highest)
    return sectioned.reshape(2, led_count, row_count, grid_size)


def plain_body(slab_phase, pupil_phase, pupil_mask, led_code, led_freq, measured):
    dev_count = lax.axis_size("pat")
    position = lax.axis_index("pat")
    slab_count, row_count, grid_size = slab_phase.shape
    col_count = grid_size // dev_count
    pattern_count, led_count = led_code.shape
    area = float(grid_size * grid_size)
    forward_set = table_set(col_count, dev_count, grid_size, -1.0)
    inverse_set = table_set(col_count, dev_count, grid_size, 1.0)
    conjugate = jnp.array([1.0, -1.0], jnp.float32)[:, None, None]
    col_freq = frequency(position * col_count + jnp.arange(col_count, dtype=jnp.int32), grid_size)
    row_freq = frequency(jnp.arange(grid_size, dtype=jnp.int32), grid_size)
    radius = col_freq[:, None] * col_freq[:, None] + row_freq[None, :] * row_freq[None, :]
    cutoff = grid_size // 2 * (grid_size // 2)
    inside = radius <= cutoff
    height = jnp.sqrt(jnp.maximum(cutoff - radius, 0).astype(jnp.float32))
    phase_shift = spread_rate * (height - grid_size // 2)
    propagator = jnp.stack(
        [jnp.where(inside, jnp.cos(phase_shift), 0.0), jnp.where(inside, jnp.sin(phase_shift), 0.0)]
    )
    opening = pupil_mask.astype(jnp.float32)
    pupil = jnp.stack([opening * jnp.cos(pupil_phase), opening * jnp.sin(pupil_phase)])
    propagator_conj = propagator * conjugate
    pupil_conj = pupil * conjugate
    row_index = position * row_count + jnp.arange(row_count, dtype=jnp.int32)
    col_index = jnp.arange(grid_size, dtype=jnp.int32)
    tilt_index = (
        led_freq[:, 0][:, None, None] * row_index[None, :, None]
        + led_freq[:, 1][:, None, None] * col_index[None, None, :]
    ) % grid_size
    tilt_angle = tilt_index.astype(jnp.float32) * (2.0 * math.pi / grid_size)
    illumination = jnp.stack([jnp.cos(tilt_angle), jnp.sin(tilt_angle)])
    transmission = jnp.stack([jnp.cos(slab_phase), jnp.sin(slab_phase)])
    group_count = 1
    group_size = led_count // group_count
    wave_groups = [illumination]
    passed_groups = []
    for slab_index in range(slab_count):
        factor = transmission[:, slab_index]
        passed = [complex_times(wave_field, factor) for wave_field in wave_groups]
        passed_groups.append(passed)
        spectral_factor = propagator if slab_index < slab_count - 1 else pupil
        wave_groups = [
            to_space(
                complex_times(to_fourier(passed_field, forward_set, dev_count), spectral_factor),
                inverse_set,
                dev_count,
            )
            for passed_field in passed
        ]
    camera = wave_groups[0]
    led_power = camera[0] * camera[0] + camera[1] * camera[1]
    code_float = led_code.astype(jnp.float32)
    pattern_power = jnp.dot(
        code_float, led_power.reshape(led_count, -1), precision=highest
    ).reshape(pattern_count, row_count, grid_size)
    counts = measured.astype(jnp.float32)
    power_sum, count_sum = lax.psum(
        (jnp.sum(pattern_power, axis=(1, 2)), jnp.sum(counts, axis=(1, 2))), "pat"
    )
    mean_power = power_sum / area
    mean_count = count_sum / area
    relative = pattern_power / mean_power[:, None, None]
    misfit = relative - counts / mean_count[:, None, None]
    coupling = lax.psum(jnp.sum(misfit * relative, axis=(1, 2)), "pat") / area
    pattern_weight = (misfit - coupling[:, None, None]) / mean_power[:, None, None]
    led_weight = jnp.dot(
        code_float.T, pattern_weight.reshape(pattern_count, -1), precision=highest
    ).reshape(led_count, row_count, grid_size)
    camera_adjoint = 2.0 * led_weight[None] * camera
    adjoint_groups = [camera_adjoint]
    gradients = [None] * slab_count
    for slab_index in range(slab_count - 1, -1, -1):
        spectral_factor = pupil_conj if slab_index == slab_count - 1 else propagator_conj
        back_groups = [
            to_space(
                complex_times(to_fourier(adjoint_field, forward_set, dev_count), spectral_factor),
                inverse_set,
                dev_count,
            )
            for adjoint_field in adjoint_groups
        ]
        gradient = jnp.zeros((row_count, grid_size), jnp.float32)
        for passed_field, back_field in zip(passed_groups[slab_index], back_groups):
            gradient = jnp.sum(
                passed_field[0] * back_field[1] - passed_field[1] * back_field[0], axis=0
            )
        gradients[slab_index] = gradient
        if slab_index > 0:
            release = transmission[:, slab_index] * conjugate
            adjoint_groups = [complex_times(back_field, release) for back_field in back_groups]
    return jnp.stack(gradients)


class Names(types.SimpleNamespace):
    pass


pupil_radius = 128
lanes = 128
f32 = jnp.float32
bf16 = jnp.bfloat16


def halves(table):
    table32 = np.asarray(table, np.float32)
    high = table32.astype(bf16)
    low = (table32 - high.astype(np.float32)).astype(bf16)
    return np.stack([high, low])


def row_tables(size, block, band_block):
    quarter = size // 4
    pos = np.arange(quarter)
    angle = 2.0 * np.pi * ((pos[:, None] * pos[None, :]) % quarter) / quarter
    cosine = np.cos(angle) / math.sqrt(size)
    sine = np.sin(angle) / math.sqrt(size)

    def forward(freqs, width):
        parts = []
        for first in range(0, len(freqs), width):
            pick = freqs[first : first + width] % quarter
            left = np.concatenate([cosine[:, pick], sine[:, pick]], 0)
            right = np.concatenate([-sine[:, pick], cosine[:, pick]], 0)
            parts.append(np.concatenate([left, right], 1))
        return np.concatenate(parts, 1)

    full = forward(pos, block)
    reach = pupil_radius // 4
    band = forward(np.arange(-reach, reach), band_block)
    theta = 2.0 * np.pi * (np.arange(4)[:, None] * pos[None, :]) / size
    twiddle = np.concatenate([np.cos(theta), np.sin(theta)], 0).astype(np.float32)
    return Names(
        full=jnp.asarray(halves(full)),
        full_inv=jnp.asarray(halves(full.T)),
        band=jnp.asarray(halves(band)),
        band_inv=jnp.asarray(halves(band.T)),
        twiddle=jnp.asarray(twiddle),
    )


def col_tables(size):
    quarter = size // 4
    pos = np.arange(quarter)
    angle = 2.0 * np.pi * ((pos[:, None] * pos[None, :]) % quarter) / quarter
    both = np.concatenate([np.cos(angle), np.sin(angle)], 0) / math.sqrt(size)
    theta = 2.0 * np.pi * (np.arange(1, 4)[:, None] * pos[None, :]) / size
    twiddle = np.stack([np.cos(theta), np.sin(theta)]).astype(np.float32)
    twiddle = np.ascontiguousarray(np.broadcast_to(twiddle[..., None], twiddle.shape + (lanes,)))
    freqs = np.arange(-pupil_radius, pupil_radius)
    angle = 2.0 * np.pi * ((np.arange(size)[:, None] * freqs[None, :]) % size) / size
    cosine = np.cos(angle) / math.sqrt(size)
    sine = np.sin(angle) / math.sqrt(size)
    band = halves(np.concatenate([cosine, sine], 1))
    band_inv = halves(np.concatenate([cosine.T, sine.T], 1))
    return Names(both=halves(both), twiddle=twiddle, band=band, band_inv=band_inv)


def split(value):
    high = value.astype(bf16)
    return high, (value - high.astype(f32)).astype(bf16)


def dot3(left, right):
    def dot(a, b):
        return jnp.dot(a, b, preferred_element_type=f32)

    return dot(left[0], right[0]) + (dot(left[0], right[1]) + dot(left[1], right[0]))


def turn(value):
    rolled = pltpu.roll(value, lanes // 2, 1)
    lane = lax.broadcasted_iota(jnp.int32, value.shape, 1)
    return jnp.where(lane < lanes // 2, rolled, -rolled)


def partner(me, step, devs):
    return lax.rem(me + step, devs)


def greet(devs):
    me = lax.axis_index("pat")
    barrier = pltpu.get_barrier_semaphore()

    def signal(step, carry):
        pl.semaphore_signal(
            barrier, inc=1, device_id=dict(pat=partner(me, step, devs)),
            device_id_type=pl.DeviceIdType.MESH,
        )
        return carry

    lax.fori_loop(1, devs, signal, 0)
    return me, barrier


def view(ref, at, part):
    return ref.at[at] if part is None else ref.at[at, part]


def remote(ref, me, dest, part, land):
    block = ref.stage if ref.same else view(ref.stage, dest, part)
    row = 0 if part is None else part
    return pltpu.make_async_remote_copy(
        src_ref=block, dst_ref=view(ref.y, land, part), send_sem=ref.sent.at[row, dest],
        recv_sem=ref.got.at[row, land], device_id=dict(pat=dest),
        device_id_type=pl.DeviceIdType.MESH,
    )


def send(ref, me, dest, part=None):
    @pl.when(dest != me)
    def _():
        remote(ref, me, dest, part, me).start()

    @pl.when(dest == me)
    def _():
        keep(ref, me, part).start()


def keep(ref, me, part):
    block = ref.stage if ref.same else view(ref.stage, me, part)
    return pltpu.make_async_copy(block, view(ref.y, me, part), ref.kept.at[0 if part is None else part])


def finish(ref, me, devs, parts=(None,)):
    for part in parts:

        def settle(step, carry):
            other = partner(me, step, devs)
            remote(ref, me, other, part, other).wait()
            return carry

        keep(ref, me, part).wait()
        lax.fori_loop(1, devs, settle, 0)


def comm_scratch(stage_shape, devs, parts=1):
    return [
        pltpu.VMEM(stage_shape, f32),
        pltpu.SemaphoreType.DMA((parts, devs)),
        pltpu.SemaphoreType.DMA((parts, devs)),
        pltpu.SemaphoreType.DMA((parts,)),
    ]


def comm_params(channel):
    return pltpu.CompilerParams(collective_id=channel, has_side_effects=True)


anywhere = pl.BlockSpec(memory_space=pl.ANY)


def row_spread(blocks, twiddle_ref):
    (r0, i0), (r1, i1), (r2, i2), (r3, i3) = blocks
    sr, si, tr, ti = r0 + r2, i0 + i2, r1 + r3, i1 + i3
    dr, di, er, ei = r0 - r2, i0 - i2, r1 - r3, i1 - i3
    mixed = [(sr + tr, si + ti), (dr + ei, di - er), (sr - tr, si - ti), (dr - ei, di + er)]
    out = [mixed[0]]
    for j in range(1, 4):
        cosine, sine = twiddle_ref[j : j + 1, :], twiddle_ref[4 + j : 5 + j, :]
        re, im = mixed[j]
        out.append((re * cosine + im * sine, im * cosine - re * sine))
    return out


def row_gather(parts, twiddle_ref):
    g = [parts[0]]
    for j in range(1, 4):
        cosine, sine = twiddle_ref[j : j + 1, :], twiddle_ref[4 + j : 5 + j, :]
        re, im = parts[j]
        g.append((re * cosine - im * sine, im * cosine + re * sine))
    (r0, i0), (r1, i1), (r2, i2), (r3, i3) = g
    sr, si, tr, ti = r0 + r2, i0 + i2, r1 + r3, i1 + i3
    dr, di, er, ei = r0 - r2, i0 - i2, r1 - r3, i1 - i3
    return [(sr + tr, si + ti), (dr - ei, di + er), (sr - tr, si - ti), (dr + ei, di - er)]


def row_kernel(spec, *refs):
    ref = Names(**dict(zip(spec.names, refs)), same=spec.kind == "stats")
    sends = spec.kind != "leave"
    if sends:
        me, barrier = greet(spec.devs)
    count, rows, quarter = spec.count, spec.rows, spec.quarter
    devs = spec.devs
    per = devs // 4
    step = 16
    total = count * rows
    hi, lo, zs, twiddle = ref.hi, ref.lo, ref.zs, ref.twiddle
    source = spec.source
    if source == "full":
        for j in range(4):
            for q in range(per):
                block = ref.x[per * j + q].reshape(total, lanes)
                high, low = split(block)
                hi[j, :total, q * lanes : (q + 1) * lanes] = high
                lo[j, :total, q * lanes : (q + 1) * lanes] = low
        for j in range(4):
            left = (hi[j, :total, :], lo[j, :total, :])
            zs[j, :total, :] = dot3(left, (ref.inv[0], ref.inv[1]))
    elif source == "band":
        for j in range(4):
            block = ref.x[per * j : per * (j + 1)].reshape(-1, total)
            zs[j, :total, :] = dot3(split(block.T), (ref.inv[0], ref.inv[1]))
    kind = spec.kind
    if kind == "stats":
        stats = [jnp.zeros((8, lanes), f32) for _ in range(spec.stat_rows)]
    if kind == "weigh":
        sums = jnp.sum(ref.stats[...], 0)
        sums = jnp.sum(sums, 1, keepdims=True)
        code = [[ref.code[p, l].astype(f32) for l in range(count)] for p in range(spec.patterns)]
        area = spec.area
        power_mean, count_mean, couple = [], [], []
        base = count + count * (count + 1) // 2
        for p in range(spec.patterns):
            mean = sum(sums[l : l + 1] * code[p][l] for l in range(count)) / area
            mean_count = sums[base + spec.patterns * count + p :][:1] / area
            square = 0.0
            at = count
            for l in range(count):
                for m in range(l, count):
                    factor = 1.0 if l == m else 2.0
                    square = square + (factor * code[p][l] * code[p][m]) * sums[at : at + 1]
                    at += 1
            cross = sum(code[p][l] * sums[base + p * count + l :][:1] for l in range(count))
            power_mean.append(mean)
            count_mean.append(mean_count)
            couple.append((square / mean / mean - cross / mean_count / mean) / area)

    def fold(value):
        total_rows = value[:8]
        for k in range(1, value.shape[0] // 8):
            total_rows = total_rows + value[8 * k : 8 * k + 8]
        out = total_rows[:, :lanes]
        for k in range(1, value.shape[1] // lanes):
            out = out + total_rows[:, lanes * k : lanes * (k + 1)]
        return out

    def chunk(i, carry):
        base_row = pl.multiple_of(i * step, step)
        here = pl.ds(base_row, step)
        fields = []
        for l in range(count):
            at = pl.ds(pl.multiple_of(l * rows + base_row, step), step)
            if source in ("full", "band"):
                parts = [(zs[j, at, :quarter], zs[j, at, quarter:]) for j in range(4)]
                fields.append(row_gather(parts, twiddle))
        cut = [slice(a * quarter, (a + 1) * quarter) for a in range(4)]

        def tilt(l, a, value, sign):
            rc, rs = ref.tilt_r[2 * l, here, :], ref.tilt_r[2 * l + 1, here, :]
            cc, cs = ref.tilt_c[2 * l : 2 * l + 1, cut[a]], ref.tilt_c[2 * l + 1 : 2 * l + 2, cut[a]]
            wide = jnp.concatenate([rc] * (quarter // lanes), 1), jnp.concatenate([rs] * (quarter // lanes), 1)
            er = wide[0] * cc - wide[1] * cs
            ei = sign * (wide[0] * cs + wide[1] * cc)
            re, im = value
            return re * er - im * ei, re * ei + im * er

        outgoing = []
        if kind == "enter":
            outgoing = [[]]
            for c in cut:
                phase = ref.slab[0, here, c]
                cosine, sine = jnp.cos(phase), jnp.sin(phase)
                ref.tr0[0, here, c] = cosine
                ref.tr0[1, here, c] = sine
                outgoing[0].append((cosine, sine))
        elif kind == "forward" or kind == "forward_band":
            for l in range(count):
                at = pl.ds(pl.multiple_of(l * rows + base_row, step), step)
                blocks = []
                for a, c in enumerate(cut):
                    tr, ti = ref.tr[0, here, c], ref.tr[1, here, c]
                    re, im = fields[l][a]
                    re, im = re * tr - im * ti, re * ti + im * tr
                    ref.passed[0, at, c] = re
                    ref.passed[1, at, c] = im
                    blocks.append((re, im) if kind == "forward" else tilt(l, a, (re, im), 1.0))
                outgoing.append(blocks)
        elif kind == "stats":
            adds = [0.0] * spec.stat_rows
            for a, c in enumerate(cut):
                power = []
                for l in range(count):
                    at = pl.ds(pl.multiple_of(l * rows + base_row, step), step)
                    re, im = fields[l][a]
                    ref.passed[0, at, c] = re
                    ref.passed[1, at, c] = im
                    power.append(re * re + im * im)
                values = list(power)
                for l in range(count):
                    for m in range(l, count):
                        values.append(power[l] * power[m])
                seen = [ref.measured[p, here, c].astype(f32) for p in range(spec.patterns)]
                for p in range(spec.patterns):
                    for l in range(count):
                        values.append(seen[p] * power[l])
                values += seen
                for k, value in enumerate(values):
                    adds[k] = adds[k] + fold(value)
            return tuple(x + y for x, y in zip(carry, adds))
        elif kind == "weigh":
            outgoing = [[] for _ in range(count)]
            for a, c in enumerate(cut):
                camera, power = [], []
                for l in range(count):
                    at = pl.ds(pl.multiple_of(l * rows + base_row, step), step)
                    re, im = ref.passed[0, at, c], ref.passed[1, at, c]
                    camera.append((re, im))
                    power.append(re * re + im * im)
                weight = [0.0] * count
                for p in range(spec.patterns):
                    lit = sum(code[p][l] * power[l] for l in range(count))
                    seen = ref.measured[p, here, c].astype(f32)
                    misfit = lit * (1.0 / power_mean[p]) - seen * (1.0 / count_mean[p])
                    pull = (misfit - couple[p]) * (1.0 / power_mean[p])
                    for l in range(count):
                        weight[l] = weight[l] + code[p][l] * pull
                for l in range(count):
                    scale = 2.0 * weight[l]
                    outgoing[l].append((scale * camera[l][0], scale * camera[l][1]))
        elif kind == "back" or kind == "back_band":
            grads = [0.0] * 4
            for l in range(count):
                at = pl.ds(pl.multiple_of(l * rows + base_row, step), step)
                blocks = []
                for a, c in enumerate(cut):
                    re, im = fields[l][a]
                    if kind == "back_band":
                        re, im = tilt(l, a, (re, im), -1.0)
                    pr, pi = ref.passed[0, at, c], ref.passed[1, at, c]
                    grads[a] = grads[a] + (pr * im - pi * re)
                    tr, ti = ref.tr[0, here, c], ref.tr[1, here, c]
                    blocks.append((re * tr + im * ti, im * tr - re * ti))
                outgoing.append(blocks)
            for a, c in enumerate(cut):
                ref.grad[here, c] = grads[a]
        elif kind == "leave":
            for a, c in enumerate(cut):
                tr, ti = ref.tr[0, here, c], ref.tr[1, here, c]
                re, im = fields[0][a]
                ref.grad[here, c] = tr * im - ti * re
        for l, blocks in enumerate(outgoing):
            at = pl.ds(pl.multiple_of(l * rows + base_row, step), step)
            for j, (re, im) in enumerate(row_spread(blocks, twiddle)):
                high, low = split(re)
                hi[j, at, :quarter] = high
                lo[j, at, :quarter] = low
                high, low = split(im)
                hi[j, at, quarter:] = high
                lo[j, at, quarter:] = low
        return carry

    if kind == "stats":
        stats = lax.fori_loop(0, rows // step, chunk, tuple(stats))
        packed = [jnp.sum(row, 0, keepdims=True) for row in stats]
        packed.append(jnp.zeros((ref.stage.shape[0] - len(packed), lanes), f32))
        packed = jnp.concatenate(packed, 0)
        ref.stage[...] = packed
        pl.semaphore_wait(barrier, devs - 1)

        def share(k, carry):
            send(ref, me, partner(me, k, devs))
            return carry

        lax.fori_loop(0, devs, share, 0)
        finish(ref, me, devs)
        return
    lax.fori_loop(0, rows // step, chunk, 0)
    if not sends:
        return
    pl.semaphore_wait(barrier, devs - 1)

    def emit(step_j, carry):
        j = lax.rem(me // per + step_j, 4)
        y = dot3((hi[j, :total, :], lo[j, :total, :]), (ref.fwd[0], ref.fwd[1]))
        if spec.target == "full":
            for q in range(per):
                ref.stage[per * j + q] = y[:, q * lanes : (q + 1) * lanes].reshape(count, rows, lanes)
        else:
            flipped = y.T
            deep = flipped.shape[0] // per
            for q in range(per):
                ref.stage[per * j + q] = flipped[q * deep : (q + 1) * deep]
        for q in range(per):
            send(ref, me, per * j + lax.rem(me + q, per))
        return carry

    lax.fori_loop(0, 4, emit, 0)
    if kind == "enter":
        pupil_out(spec, ref, me)
        prepare(spec, ref, me)
        pupil_in(spec, ref, me)
    finish(ref, me, devs)


def pupil_copy(spec, ref, j, dest):
    return pltpu.make_async_remote_copy(
        src_ref=ref.own.at[j], dst_ref=ref.pupil, send_sem=ref.psent.at[j], recv_sem=ref.pgot,
        device_id=dict(pat=dest), device_id_type=pl.DeviceIdType.MESH,
    )


def pupil_out(spec, ref, me):
    per = spec.devs // 4
    for q in range(per):

        @pl.when(me == spec.owners[q])
        def _():
            for j in range(4):
                pupil_copy(spec, ref, j, per * j + q).start()


def pupil_in(spec, ref, me):
    per = spec.devs // 4
    pupil_copy(spec, ref, 0, partner(me, 1, spec.devs)).wait_recv()
    for q in range(per):

        @pl.when(me == spec.owners[q])
        def _():
            for j in range(4):
                pupil_copy(spec, ref, j, per * j + q).wait_send()


def prepare(spec, ref, me):
    size, quarter = 4 * spec.quarter, spec.quarter
    per, half, step = spec.devs // 4, lanes // 2, 16
    cutoff = size // 2 * (size // 2)

    def phases(i, carry):
        here = pl.ds(pl.multiple_of(i * step, step), step)
        for s, out in ((1, ref.tr1), (2, ref.tr2)):
            phase = ref.slab[s, here, :]
            out[0, here, :] = jnp.cos(phase)
            out[1, here, :] = jnp.sin(phase)
        return carry

    lax.fori_loop(0, spec.rows // step, phases, 0)

    def centred(index):
        return jnp.where(index >= size // 2, index - size, index)

    def spectrum(i, carry):
        here = pl.ds(pl.multiple_of(i * step, step), step)
        row = lax.broadcasted_iota(jnp.int32, (step, lanes), 0) + i * step
        lane = lax.broadcasted_iota(jnp.int32, (step, lanes), 1)
        lane = jnp.where(lane < half, lane, lane - half)
        col = 4 * (lax.rem(me, per) * half + lane) + me // per
        for l in range(spec.leds):
            v = centred(col + ref.freq[l, 1])
            for j in range(4):
                u = centred(4 * row + j + ref.freq[l, 0])
                radius = u * u + v * v
                inside = radius <= cutoff
                height = jnp.sqrt(jnp.maximum(cutoff - radius, 0).astype(f32))
                shift = spread_rate * (height - float(size // 2))
                ref.prop[0, l, j, here, :] = jnp.where(inside, jnp.cos(shift), 0.0)
                ref.prop[1, l, j, here, :] = jnp.where(inside, jnp.sin(shift), 0.0)
        return carry

    lax.fori_loop(0, quarter // step, spectrum, 0)


def run_rows(channel, kind, source, target, dims, inputs, outputs):
    spec = Names(**vars(dims), kind=kind, source=source, target=target)
    count = spec.count
    total = count * spec.rows
    wide = 2 * spec.quarter
    names = list(inputs) + list(outputs) + ["hi", "lo", "zs"]
    sends = "y" in outputs
    comm = []
    if sends:
        names += ["stage", "sent", "got", "kept"]
        shape = outputs["y"]
        comm = comm_scratch(shape[1:] if kind == "stats" else shape, spec.devs)
    if kind == "enter":
        names += ["psent", "pgot"]
        comm += [pltpu.SemaphoreType.DMA((4,)), pltpu.SemaphoreType.DMA]
    spec.names = names
    vmem = pl.BlockSpec(memory_space=pltpu.VMEM)
    in_specs = [
        pl.BlockSpec(memory_space=pltpu.SMEM) if name in ("code", "freq") else vmem for name in inputs
    ]
    return pl.pallas_call(
        functools.partial(row_kernel, spec),
        out_shape=[jax.ShapeDtypeStruct(shape, f32) for shape in outputs.values()],
        in_specs=in_specs,
        out_specs=[anywhere if name in ("y", "pupil") else vmem for name in outputs],
        scratch_shapes=[
            pltpu.VMEM((4, total, wide), bf16),
            pltpu.VMEM((4, total, wide), bf16),
            pltpu.VMEM((4, total, wide), f32),
        ]
        + comm,
        compiler_params=comm_params(channel) if sends else None,
        name="rows_" + kind,
    )(*inputs.values())


def col_kernel(spec, x_ref, p_ref, w_ref, t_ref, y_ref, hi, lo, zs, stage, sent, got, kept):
    ref = Names(y=y_ref, stage=stage, sent=sent, got=got, kept=kept, same=False)
    me, barrier = greet(spec.devs)
    rows, quarter, devs = spec.rows, spec.quarter, spec.devs
    count_in, count_out, sign = spec.count_in, spec.count_out, spec.sign
    count = p_ref.shape[1]
    per = devs // 4
    weights = (w_ref[0], w_ref[1])
    wide_out = count_out * lanes

    def spread(l):
        at = slice(l * lanes, (l + 1) * lanes)

        def step(i, carry):
            here = pl.ds(pl.multiple_of(i * rows, rows), rows)
            x0, x1, x2, x3 = [x_ref[per * a + i, l] for a in range(4)]
            s, t, d, e = x0 + x2, x1 + x3, x0 - x2, turn(x1 - x3)
            for j, value in enumerate((s + t, d + e, s - t, d - e)):
                if j:
                    value = value * t_ref[0, j - 1, here, :] + turn(value) * t_ref[1, j - 1, here, :]
                high, low = split(value)
                hi[j, here, at] = high
                lo[j, here, at] = low
            return carry

        lax.fori_loop(0, per, step, 0)

    def spectra(first, number):
        span = slice(first * lanes, (first + number) * lanes)
        found = []
        for j in range(4):
            y = dot3(weights, (hi[j, :, span], lo[j, :, span]))
            found.append([])
            for l in range(number):
                at = slice(l * lanes, (l + 1) * lanes)
                found[j].append(y[:quarter, at] + turn(y[quarter:, at]))
        return found

    def pass_on(l, fields):
        at = slice(l * lanes, (l + 1) * lanes)
        for j in range(4):
            high, low = split(fields[j])
            hi[j, :, at] = high
            lo[j, :, at] = low
        for j in range(4):
            y = dot3(weights, (hi[j, :, at], lo[j, :, at]))
            value = y[:quarter] - turn(y[quarter:])
            if j:
                value = value * t_ref[0, j - 1] - turn(value) * t_ref[1, j - 1]
            zs[j, :, at] = value
        if l == 0:
            pl.semaphore_wait(barrier, devs - 1)

        def gather(step, carry):
            i = lax.rem(me + step, per)
            here = pl.ds(pl.multiple_of(i * rows, rows), rows)
            g0, g1, g2, g3 = [zs[j, here, at] for j in range(4)]
            s, t, d, e = g0 + g2, g1 + g3, g0 - g2, turn(g1 - g3)
            for a, value in enumerate((s + t, d - e, s - t, d + e)):
                stage[per * a + i, l] = value
            for a in range(4):
                send(ref, me, lax.rem(me // per + a, 4) * per + i, l)
            return carry

        lax.fori_loop(0, per, gather, 0)

    def shaped(z, l, j):
        return z * p_ref[0, l, j] - sign * (turn(z) * p_ref[1, l, j])

    if count_in == count_out:
        for l in range(count):
            spread(l)
            z = spectra(l, 1)
            pass_on(l, [shaped(z[j][0], l, j) for j in range(4)])
    else:
        for l in range(count_in):
            spread(l)
        z = spectra(0, count_in)
        if count_out == 1:
            pass_on(0, [sum(shaped(z[j][l], l, j) for l in range(count)) for j in range(4)])
        else:
            for j in range(4):
                zs[j, :, wide_out:] = z[j][0]
            for l in range(count):
                pass_on(l, [shaped(zs[j, :, wide_out:], l, j) for j in range(4)])
    finish(ref, me, devs, tuple(range(count_out)))


def run_cols(channel, x, prop, tables, dims, count_in, count_out, sign):
    spec = Names(**vars(dims), count_in=count_in, count_out=count_out, sign=sign)
    rows, quarter, devs = dims.rows, dims.quarter, dims.devs
    wide = max(count_in, count_out) * lanes
    vmem = pl.BlockSpec(memory_space=pltpu.VMEM)
    return pl.pallas_call(
        functools.partial(col_kernel, spec),
        out_shape=jax.ShapeDtypeStruct((devs, count_out, rows, lanes), f32),
        in_specs=[vmem] * 4,
        out_specs=anywhere,
        scratch_shapes=[
            pltpu.VMEM((4, quarter, wide), bf16),
            pltpu.VMEM((4, quarter, wide), bf16),
            pltpu.VMEM((4, quarter, wide + lanes), f32),
        ]
        + comm_scratch((devs, count_out, rows, lanes), devs, count_out),
        compiler_params=comm_params(channel),
        name="cols",
    )(x, prop, jnp.asarray(tables.both), jnp.asarray(tables.twiddle))


def band_kernel(spec, x_ref, p_ref, w_ref, v_ref, y_ref, stage, sent, got, kept):
    ref = Names(y=y_ref, stage=stage, sent=sent, got=got, kept=kept, same=False)
    me, barrier = greet(spec.devs)
    devs, sign, count = spec.devs, spec.sign, spec.count
    half = lanes // 2
    lane = lax.broadcasted_iota(jnp.int32, x_ref.shape[1:], 1)
    pieces = [[], []]
    for s in range(0, devs, 2):
        even, odd = x_ref[s], x_ref[s + 1]
        pieces[0].append(jnp.where(lane < half, even, pltpu.roll(odd, half, 1)))
        pieces[1].append(jnp.where(lane < half, pltpu.roll(even, half, 1), odd))
    field = jnp.concatenate([jnp.concatenate(p, 1) for p in pieces], 0)
    wide = w_ref.shape[2] // 2
    deep = v_ref.shape[2] // 2
    cols = x_ref.shape[1] // 2
    both = dot3(split(field), (w_ref[0], w_ref[1]))
    scaled = []
    for l in range(count):
        re = slice(2 * l * cols, (2 * l + 1) * cols)
        im = slice((2 * l + 1) * cols, (2 * l + 2) * cols)
        yr = both[re, :wide] + both[im, wide:]
        yi = both[im, :wide] - both[re, wide:]
        pr, pi = p_ref[0], sign * p_ref[1]
        scaled += [yr * pr - yi * pi, yr * pi + yi * pr]
    both = dot3(split(jnp.concatenate(scaled, 0)), (v_ref[0], v_ref[1]))
    out = []
    for l in range(count):
        re = slice(2 * l * cols, (2 * l + 1) * cols)
        im = slice((2 * l + 1) * cols, (2 * l + 2) * cols)
        out.append(
            jnp.concatenate(
                [both[re, :deep] - both[im, deep:], both[im, :deep] + both[re, deep:]], 0
            )
        )
    for s in range(0, devs, 2):
        at = slice(s * half, s * half + lanes)
        first, second = out[0][:, at], out[1][:, at]
        stage[s] = jnp.where(lane < half, first, pltpu.roll(second, half, 1))
        stage[s + 1] = jnp.where(lane < half, pltpu.roll(first, half, 1), second)
    pl.semaphore_wait(barrier, devs - 1)

    def share(k, carry):
        send(ref, me, partner(me, k, devs))
        return carry

    lax.fori_loop(0, devs, share, 0)
    finish(ref, me, devs)


def run_band(channel, x, pupil, tables, dims, sign):
    vmem = pl.BlockSpec(memory_space=pltpu.VMEM)
    return pl.pallas_call(
        functools.partial(band_kernel, Names(**vars(dims), sign=sign)),
        out_shape=jax.ShapeDtypeStruct(x.shape, f32),
        in_specs=[vmem] * 4,
        out_specs=anywhere,
        scratch_shapes=comm_scratch(x.shape, dims.devs),
        compiler_params=comm_params(channel),
        name="pupil_cols",
    )(x, pupil, jnp.asarray(tables.band), jnp.asarray(tables.band_inv))


def body(slab_phase, pupil_phase, pupil_mask, led_code, led_freq, measured):
    devs = lax.axis_size("pat")
    position = lax.axis_index("pat")
    slab_count, rows, size = slab_phase.shape
    patterns, count = led_code.shape
    quarter, cols, per = size // 4, size // devs, devs // 4
    band = 2 * pupil_radius
    band_cols = band // devs
    dims = Names(
        count=count, rows=rows, quarter=quarter, devs=devs, patterns=patterns,
        area=float(size * size),
    )
    rt = row_tables(size, cols, band_cols)
    ct = col_tables(size)
    shape_full = (devs, count, rows, lanes)
    shape_band = (devs, 2 * band_cols, count * rows)
    shape_field = (2, count * rows, size)
    twiddle, table = rt.twiddle, rt

    def near(x):
        return jnp.concatenate([x[:, size - pupil_radius :], x[:, :pupil_radius]], 1)

    opening, phase = near(pupil_mask).astype(f32), near(pupil_phase)
    own = jnp.stack([opening * jnp.cos(phase), opening * jnp.sin(phase)])
    own = jnp.transpose(own.reshape(2, cols // 4, 4, band), (2, 0, 1, 3))
    owners = [(q - pupil_radius // cols) % devs for q in range(per)]

    def wave(freq, index):
        turns = (freq[:, None] * index[None, :]) % size
        angle = turns.astype(f32) * (2.0 * math.pi / size)
        return jnp.stack([jnp.cos(angle), jnp.sin(angle)], 1).reshape(2 * count, -1)

    tilt_c = wave(led_freq[:, 1], jnp.arange(size, dtype=jnp.int32))
    tilt_r = wave(led_freq[:, 0], position * rows + jnp.arange(rows, dtype=jnp.int32))
    tilt_r = jnp.broadcast_to(tilt_r[:, :, None], (2 * count, rows, lanes))
    tilts = dict(tilt_r=tilt_r, tilt_c=tilt_c)
    full_both = dict(inv=table.full_inv, fwd=table.full, twiddle=twiddle)

    one = Names(**{**vars(dims), **dict(count=1)}, leds=count, owners=owners)
    shape_trans = (2, rows, size)
    y, tr0, tr1, tr2, prop, pupil = run_rows(
        7, "enter", None, "full", one,
        dict(slab=slab_phase, own=own, freq=led_freq, fwd=table.full, twiddle=twiddle),
        dict(
            y=(devs, 1, rows, lanes), tr0=shape_trans, tr1=shape_trans, tr2=shape_trans,
            prop=(2, count, 4, quarter, lanes), pupil=(2, band_cols, band),
        ),
    )
    transmission = [tr0, tr1, tr2]
    x = run_cols(1, y, prop, ct, dims, 1, count, 1.0)
    y, passed1 = run_rows(
        8, "forward", "full", "full", dims, dict(x=x, tr=transmission[1], **full_both),
        dict(y=shape_full, passed=shape_field),
    )
    x = run_cols(2, y, prop, ct, dims, count, count, 1.0)
    y, passed2 = run_rows(
        9, "forward_band", "full", "band", dims,
        dict(x=x, tr=transmission[2], inv=table.full_inv, fwd=table.band, twiddle=twiddle, **tilts),
        dict(y=shape_band, passed=shape_field),
    )
    x = run_band(3, y, pupil, ct, dims, 1.0)
    stat_rows = count + count * (count + 1) // 2 + patterns * count + patterns
    dims.stat_rows = stat_rows
    camera, sums = run_rows(
        10, "stats", "band", None, dims,
        dict(x=x, inv=table.band_inv, twiddle=twiddle, measured=measured),
        dict(passed=shape_field, y=(devs, -(-stat_rows // 8) * 8, lanes)),
    )
    (y,) = run_rows(
        11, "weigh", None, "band", dims,
        dict(stats=sums, code=led_code, passed=camera, measured=measured, fwd=table.band, twiddle=twiddle),
        dict(y=shape_band),
    )
    x = run_band(4, y, pupil, ct, dims, -1.0)
    y, grad2 = run_rows(
        12, "back_band", "band", "full", dims,
        dict(x=x, tr=transmission[2], passed=passed2, inv=table.band_inv, fwd=table.full, twiddle=twiddle, **tilts),
        dict(y=shape_full, grad=(rows, size)),
    )
    x = run_cols(5, y, prop, ct, dims, count, count, -1.0)
    y, grad1 = run_rows(
        13, "back", "full", "full", dims,
        dict(x=x, tr=transmission[1], passed=passed1, **full_both),
        dict(y=shape_full, grad=(rows, size)),
    )
    x = run_cols(6, y, prop, ct, dims, count, 1, -1.0)
    (grad0,) = run_rows(
        14, "leave", "full", None, one,
        dict(x=x, tr=transmission[0], inv=table.full_inv, twiddle=twiddle),
        dict(grad=(rows, size)),
    )
    return jnp.stack([grad0, grad1, grad2])


def solution(mesh):
    in_specs = (
        P("tiles", "pat", None),
        P("pat", None),
        P("pat", None),
        P(),
        P(),
        P("tiles", "pat", None),
    )
    out_specs = P("tiles", "pat", None)
    def run(slab_phase, *others):
        devs = mesh.shape["pat"]
        size, count = slab_phase.shape[-1], others[2].shape[1]
        fits = 2 * size == lanes * devs and count * size == lanes * devs and slab_phase.shape[0] == 3 * mesh.shape["tiles"]
        inner = body if fits else plain_body
        return jax.shard_map(inner, mesh=mesh, in_specs=in_specs, out_specs=out_specs, check_vma=False)(
            slab_phase, *others
        )

    return run
```

```python
import functools
import math
import types

import jax
import jax.numpy as jnp
import numpy as np
from jax import lax
from jax.experimental import pallas as pl
from jax.experimental.pallas import tpu as pltpu
from jax.sharding import PartitionSpec as P

spread_rate = 0.3
highest = lax.Precision.HIGHEST


def frequency(grid_index, grid_size):
    return (grid_index + grid_size // 2) % grid_size - grid_size // 2


def complex_times(values, factor):
    real_part = values[0] * factor[0] - values[1] * factor[1]
    imag_part = values[0] * factor[1] + values[1] * factor[0]
    return jnp.stack([real_part, imag_part])


def dft_block(length, direction, norm_factor):
    grid_index = jnp.arange(length, dtype=jnp.int32)
    angles = (grid_index[:, None] * grid_index[None, :] % length).astype(jnp.float32) * (
        2.0 * math.pi / length
    )
    cosine = jnp.cos(angles) * norm_factor
    signed_sine = direction * jnp.sin(angles) * norm_factor
    real_rows = jnp.stack([cosine, signed_sine], 1)
    imag_rows = jnp.stack([-signed_sine, cosine], 1)
    return jnp.stack([real_rows, imag_rows], 0)


def twiddle_table(short_size, long_size, grid_size, direction):
    short_index = jnp.arange(short_size, dtype=jnp.int32)
    long_index = jnp.arange(long_size, dtype=jnp.int32)
    angles = (short_index[:, None] * long_index[None, :] % grid_size).astype(jnp.float32) * (
        2.0 * math.pi / grid_size
    )
    return jnp.stack([jnp.cos(angles), direction * jnp.sin(angles)])


def table_set(col_count, dev_count, grid_size, direction):
    short_table = dft_block(col_count, direction, 1.0)
    long_table = dft_block(dev_count, direction, 1.0 / math.sqrt(grid_size))
    return (short_table, long_table, twiddle_table(col_count, dev_count, grid_size, direction))


def to_fourier(wave_field, tables, dev_count):
    short_table, long_table, twiddles = tables
    led_count = wave_field.shape[1]
    row_count = wave_field.shape[2]
    grid_size = wave_field.shape[3]
    col_count = grid_size // dev_count
    shaped = wave_field.reshape(2, led_count, row_count, col_count, dev_count)
    sectioned = jnp.einsum("zlrmq,zmwc->wlrcq", shaped, short_table, precision=highest)
    sectioned = complex_times(sectioned, twiddles)
    outgoing = jnp.einsum("wlrcq,wqvd->dvlcr", sectioned, long_table, precision=highest)
    incoming = lax.all_to_all(
        outgoing.reshape(dev_count, -1), "pat", split_axis=0, concat_axis=0, tiled=True
    )
    incoming = incoming.reshape(dev_count, 2, led_count, col_count, row_count)
    sectioned = jnp.einsum("swlcr,wsvj->vlcrj", incoming, long_table, precision=highest)
    sectioned = complex_times(sectioned, twiddles)
    sectioned = jnp.einsum("wlcrj,wrvh->vlchj", sectioned, short_table, precision=highest)
    return sectioned.reshape(2, led_count, col_count, grid_size)


def to_space(spectrum, tables, dev_count):
    short_table, long_table, twiddles = tables
    led_count = spectrum.shape[1]
    col_count = spectrum.shape[2]
    grid_size = spectrum.shape[3]
    row_count = grid_size // dev_count
    shaped = spectrum.reshape(2, led_count, col_count, row_count, dev_count)
    sectioned = jnp.einsum("zlcmq,zmwr->wlcrq", shaped, short_table, precision=highest)
    sectioned = complex_times(sectioned, twiddles)
    outgoing = jnp.einsum("wlcrq,wqvd->dvlcr", sectioned, long_table, precision=highest)
    incoming = lax.all_to_all(
        outgoing.reshape(dev_count, -1), "pat", split_axis=0, concat_axis=0, tiled=True
    )
    incoming = incoming.reshape(dev_count, 2, led_count, col_count, row_count)
    sectioned = jnp.einsum("swlcr,wsvj->vlrcj", incoming, long_table, precision=highest)
    sectioned = complex_times(sectioned, twiddles)
    sectioned = jnp.einsum("wlrcj,wcvh->vlrhj", sectioned, short_table, precision=highest)
    return sectioned.reshape(2, led_count, row_count, grid_size)


def plain_body(slab_phase, pupil_phase, pupil_mask, led_code, led_freq, measured):
    dev_count = lax.axis_size("pat")
    position = lax.axis_index("pat")
    slab_count, row_count, grid_size = slab_phase.shape
    col_count = grid_size // dev_count
    pattern_count, led_count = led_code.shape
    area = float(grid_size * grid_size)
    forward_set = table_set(col_count, dev_count, grid_size, -1.0)
    inverse_set = table_set(col_count, dev_count, grid_size, 1.0)
    conjugate = jnp.array([1.0, -1.0], jnp.float32)[:, None, None]
    col_freq = frequency(position * col_count + jnp.arange(col_count, dtype=jnp.int32), grid_size)
    row_freq = frequency(jnp.arange(grid_size, dtype=jnp.int32), grid_size)
    radius = col_freq[:, None] * col_freq[:, None] + row_freq[None, :] * row_freq[None, :]
    cutoff = grid_size // 2 * (grid_size // 2)
    inside = radius <= cutoff
    height = jnp.sqrt(jnp.maximum(cutoff - radius, 0).astype(jnp.float32))
    phase_shift = spread_rate * (height - grid_size // 2)
    propagator = jnp.stack(
        [jnp.where(inside, jnp.cos(phase_shift), 0.0), jnp.where(inside, jnp.sin(phase_shift), 0.0)]
    )
    opening = pupil_mask.astype(jnp.float32)
    pupil = jnp.stack([opening * jnp.cos(pupil_phase), opening * jnp.sin(pupil_phase)])
    propagator_conj = propagator * conjugate
    pupil_conj = pupil * conjugate
    row_index = position * row_count + jnp.arange(row_count, dtype=jnp.int32)
    col_index = jnp.arange(grid_size, dtype=jnp.int32)
    tilt_index = (
        led_freq[:, 0][:, None, None] * row_index[None, :, None]
        + led_freq[:, 1][:, None, None] * col_index[None, None, :]
    ) % grid_size
    tilt_angle = tilt_index.astype(jnp.float32) * (2.0 * math.pi / grid_size)
    illumination = jnp.stack([jnp.cos(tilt_angle), jnp.sin(tilt_angle)])
    transmission = jnp.stack([jnp.cos(slab_phase), jnp.sin(slab_phase)])
    group_count = 1
    group_size = led_count // group_count
    wave_groups = [illumination]
    passed_groups = []
    for slab_index in range(slab_count):
        factor = transmission[:, slab_index]
        passed = [complex_times(wave_field, factor) for wave_field in wave_groups]
        passed_groups.append(passed)
        spectral_factor = propagator if slab_index < slab_count - 1 else pupil
        wave_groups = [
            to_space(
                complex_times(to_fourier(passed_field, forward_set, dev_count), spectral_factor),
                inverse_set,
                dev_count,
            )
            for passed_field in passed
        ]
    camera = wave_groups[0]
    led_power = camera[0] * camera[0] + camera[1] * camera[1]
    code_float = led_code.astype(jnp.float32)
    pattern_power = jnp.dot(
        code_float, led_power.reshape(led_count, -1), precision=highest
    ).reshape(pattern_count, row_count, grid_size)
    counts = measured.astype(jnp.float32)
    power_sum, count_sum = lax.psum(
        (jnp.sum(pattern_power, axis=(1, 2)), jnp.sum(counts, axis=(1, 2))), "pat"
    )
    mean_power = power_sum / area
    mean_count = count_sum / area
    relative = pattern_power / mean_power[:, None, None]
    misfit = relative - counts / mean_count[:, None, None]
    coupling = lax.psum(jnp.sum(misfit * relative, axis=(1, 2)), "pat") / area
    pattern_weight = (misfit - coupling[:, None, None]) / mean_power[:, None, None]
    led_weight = jnp.dot(
        code_float.T, pattern_weight.reshape(pattern_count, -1), precision=highest
    ).reshape(led_count, row_count, grid_size)
    camera_adjoint = 2.0 * led_weight[None] * camera
    adjoint_groups = [camera_adjoint]
    gradients = [None] * slab_count
    for slab_index in range(slab_count - 1, -1, -1):
        spectral_factor = pupil_conj if slab_index == slab_count - 1 else propagator_conj
        back_groups = [
            to_space(
                complex_times(to_fourier(adjoint_field, forward_set, dev_count), spectral_factor),
                inverse_set,
                dev_count,
            )
            for adjoint_field in adjoint_groups
        ]
        gradient = jnp.zeros((row_count, grid_size), jnp.float32)
        for passed_field, back_field in zip(passed_groups[slab_index], back_groups):
            gradient = jnp.sum(
                passed_field[0] * back_field[1] - passed_field[1] * back_field[0], axis=0
            )
        gradients[slab_index] = gradient
        if slab_index > 0:
            release = transmission[:, slab_index] * conjugate
            adjoint_groups = [complex_times(back_field, release) for back_field in back_groups]
    return jnp.stack(gradients)


class Names(types.SimpleNamespace):
    pass


pupil_radius = 128
lanes = 128
f32 = jnp.float32
bf16 = jnp.bfloat16


def halves(table):
    table32 = np.asarray(table, np.float32)
    high = table32.astype(bf16)
    low = (table32 - high.astype(np.float32)).astype(bf16)
    return np.stack([high, low])


def row_tables(size, block, band_block):
    quarter = size // 4
    pos = np.arange(quarter)
    angle = 2.0 * np.pi * ((pos[:, None] * pos[None, :]) % quarter) / quarter
    cosine = np.cos(angle) / math.sqrt(size)
    sine = np.sin(angle) / math.sqrt(size)

    def forward(freqs, width):
        parts = []
        for first in range(0, len(freqs), width):
            pick = freqs[first : first + width] % quarter
            left = np.concatenate([cosine[:, pick], sine[:, pick]], 0)
            right = np.concatenate([-sine[:, pick], cosine[:, pick]], 0)
            parts.append(np.concatenate([left, right], 1))
        return np.concatenate(parts, 1)

    full = forward(pos, block)
    reach = pupil_radius // 4
    band = forward(np.arange(-reach, reach), band_block)
    theta = 2.0 * np.pi * (np.arange(4)[:, None] * pos[None, :]) / size
    twiddle = np.concatenate([np.cos(theta), np.sin(theta)], 0).astype(np.float32)
    return Names(
        full=jnp.asarray(halves(full)),
        full_inv=jnp.asarray(halves(full.T)),
        band=jnp.asarray(halves(band)),
        band_inv=jnp.asarray(halves(band.T)),
        twiddle=jnp.asarray(twiddle),
    )


def col_tables(size):
    quarter = size // 4
    pos = np.arange(quarter)
    angle = 2.0 * np.pi * ((pos[:, None] * pos[None, :]) % quarter) / quarter
    both = np.concatenate([np.cos(angle), np.sin(angle)], 0) / math.sqrt(size)
    theta = 2.0 * np.pi * (np.arange(1, 4)[:, None] * pos[None, :]) / size
    twiddle = np.stack([np.cos(theta), np.sin(theta)]).astype(np.float32)
    twiddle = np.ascontiguousarray(np.broadcast_to(twiddle[..., None], twiddle.shape + (lanes,)))
    freqs = np.arange(-pupil_radius, pupil_radius)
    angle = 2.0 * np.pi * ((np.arange(size)[:, None] * freqs[None, :]) % size) / size
    cosine = np.cos(angle) / math.sqrt(size)
    sine = np.sin(angle) / math.sqrt(size)
    band = halves(np.concatenate([cosine, sine], 1))
    band_inv = halves(np.concatenate([cosine.T, sine.T], 1))
    return Names(both=halves(both), twiddle=twiddle, band=band, band_inv=band_inv)


def split(value):
    high = value.astype(bf16)
    return high, (value - high.astype(f32)).astype(bf16)


def dot3(left, right):
    def dot(a, b):
        return jnp.dot(a, b, preferred_element_type=f32)

    return dot(left[0], right[0]) + (dot(left[0], right[1]) + dot(left[1], right[0]))


def turn(value):
    rolled = pltpu.roll(value, lanes // 2, 1)
    lane = lax.broadcasted_iota(jnp.int32, value.shape, 1)
    return jnp.where(lane < lanes // 2, rolled, -rolled)


def partner(me, step, devs):
    return lax.rem(me + step, devs)


def greet(devs):
    me = lax.axis_index("pat")
    barrier = pltpu.get_barrier_semaphore()

    def signal(step, carry):
        pl.semaphore_signal(
            barrier, inc=1, device_id=dict(pat=partner(me, step, devs)),
            device_id_type=pl.DeviceIdType.MESH,
        )
        return carry

    lax.fori_loop(1, devs, signal, 0)
    return me, barrier


def view(ref, at, part):
    return ref.at[at] if part is None else ref.at[at, part]


def remote(ref, me, dest, part, land):
    block = ref.stage if ref.same else view(ref.stage, dest, part)
    row = 0 if part is None else part
    return pltpu.make_async_remote_copy(
        src_ref=block, dst_ref=view(ref.y, land, part), send_sem=ref.sent.at[row, dest],
        recv_sem=ref.got.at[row, land], device_id=dict(pat=dest),
        device_id_type=pl.DeviceIdType.MESH,
    )


def send(ref, me, dest, part=None):
    @pl.when(dest != me)
    def _():
        remote(ref, me, dest, part, me).start()

    @pl.when(dest == me)
    def _():
        keep(ref, me, part).start()


def groups(me, per):
    z = me // per
    return [lax.rem(z + 2, 4), 3 - z, z + 1 - 2 * lax.rem(z, 2), z]


def send_all(ref, me, devs, part=None):
    per = devs // 4
    for j in groups(me, per):

        def share(q, carry):
            send(ref, me, per * j + lax.rem(me + q, per), part)
            return carry

        lax.fori_loop(0, per, share, 0)


def keep(ref, me, part):
    block = ref.stage if ref.same else view(ref.stage, me, part)
    return pltpu.make_async_copy(block, view(ref.y, me, part), ref.kept.at[0 if part is None else part])


def finish(ref, me, devs, parts=(None,)):
    for part in parts:

        def settle(step, carry):
            other = partner(me, step, devs)
            remote(ref, me, other, part, other).wait()
            return carry

        keep(ref, me, part).wait()
        lax.fori_loop(1, devs, settle, 0)


def comm_scratch(stage_shape, devs, parts=1):
    return [
        pltpu.VMEM(stage_shape, f32),
        pltpu.SemaphoreType.DMA((parts, devs)),
        pltpu.SemaphoreType.DMA((parts, devs)),
        pltpu.SemaphoreType.DMA((parts,)),
    ]


def comm_params(channel):
    return pltpu.CompilerParams(collective_id=channel, has_side_effects=True)


anywhere = pl.BlockSpec(memory_space=pl.ANY)


def row_spread(blocks, twiddle_ref):
    (r0, i0), (r1, i1), (r2, i2), (r3, i3) = blocks
    sr, si, tr, ti = r0 + r2, i0 + i2, r1 + r3, i1 + i3
    dr, di, er, ei = r0 - r2, i0 - i2, r1 - r3, i1 - i3
    mixed = [(sr + tr, si + ti), (dr + ei, di - er), (sr - tr, si - ti), (dr - ei, di + er)]
    out = [mixed[0]]
    for j in range(1, 4):
        cosine, sine = twiddle_ref[j : j + 1, :], twiddle_ref[4 + j : 5 + j, :]
        re, im = mixed[j]
        out.append((re * cosine + im * sine, im * cosine - re * sine))
    return out


def row_gather(parts, twiddle_ref):
    g = [parts[0]]
    for j in range(1, 4):
        cosine, sine = twiddle_ref[j : j + 1, :], twiddle_ref[4 + j : 5 + j, :]
        re, im = parts[j]
        g.append((re * cosine - im * sine, im * cosine + re * sine))
    (r0, i0), (r1, i1), (r2, i2), (r3, i3) = g
    sr, si, tr, ti = r0 + r2, i0 + i2, r1 + r3, i1 + i3
    dr, di, er, ei = r0 - r2, i0 - i2, r1 - r3, i1 - i3
    return [(sr + tr, si + ti), (dr - ei, di + er), (sr - tr, si - ti), (dr + ei, di - er)]


def row_kernel(spec, *refs):
    ref = Names(**dict(zip(spec.names, refs)), same=spec.kind == "stats")
    sends = spec.kind != "leave"
    if sends:
        me, barrier = greet(spec.devs)
    count, rows, quarter = spec.count, spec.rows, spec.quarter
    devs = spec.devs
    per = devs // 4
    step = 16
    total = count * rows
    hi, lo, zs, twiddle = ref.hi, ref.lo, ref.zs, ref.twiddle
    source = spec.source
    if source == "full":
        for j in range(4):
            for q in range(per):
                block = ref.x[per * j + q].reshape(total, lanes)
                high, low = split(block)
                hi[j, :total, q * lanes : (q + 1) * lanes] = high
                lo[j, :total, q * lanes : (q + 1) * lanes] = low
        for j in range(4):
            left = (hi[j, :total, :], lo[j, :total, :])
            zs[j, :total, :] = dot3(left, (ref.inv[0], ref.inv[1]))
    elif source == "band":
        for j in range(4):
            block = ref.x[per * j : per * (j + 1)].reshape(-1, total)
            zs[j, :total, :] = dot3(split(block.T), (ref.inv[0], ref.inv[1]))
    kind = spec.kind
    if kind == "stats":
        stats = [jnp.zeros((8, lanes), f32) for _ in range(spec.stat_rows)]
    if kind == "weigh":
        sums = jnp.sum(ref.stats[...], 0)
        sums = jnp.sum(sums, 1, keepdims=True)
        code = [[ref.code[p, l].astype(f32) for l in range(count)] for p in range(spec.patterns)]
        area = spec.area
        power_mean, count_mean, couple = [], [], []
        base = count + count * (count + 1) // 2
        for p in range(spec.patterns):
            mean = sum(sums[l : l + 1] * code[p][l] for l in range(count)) / area
            mean_count = sums[base + spec.patterns * count + p :][:1] / area
            square = 0.0
            at = count
            for l in range(count):
                for m in range(l, count):
                    factor = 1.0 if l == m else 2.0
                    square = square + (factor * code[p][l] * code[p][m]) * sums[at : at + 1]
                    at += 1
            cross = sum(code[p][l] * sums[base + p * count + l :][:1] for l in range(count))
            power_mean.append(mean)
            count_mean.append(mean_count)
            couple.append((square / mean / mean - cross / mean_count / mean) / area)

    def fold(value):
        total_rows = value[:8]
        for k in range(1, value.shape[0] // 8):
            total_rows = total_rows + value[8 * k : 8 * k + 8]
        out = total_rows[:, :lanes]
        for k in range(1, value.shape[1] // lanes):
            out = out + total_rows[:, lanes * k : lanes * (k + 1)]
        return out

    def chunk(i, carry):
        base_row = pl.multiple_of(i * step, step)
        here = pl.ds(base_row, step)
        fields = []
        for l in range(count):
            at = pl.ds(pl.multiple_of(l * rows + base_row, step), step)
            if source in ("full", "band"):
                parts = [(zs[j, at, :quarter], zs[j, at, quarter:]) for j in range(4)]
                fields.append(row_gather(parts, twiddle))
        cut = [slice(a * quarter, (a + 1) * quarter) for a in range(4)]

        def tilt(l, a, value, sign):
            rc, rs = ref.tilt_r[2 * l, here, :], ref.tilt_r[2 * l + 1, here, :]
            cc, cs = ref.tilt_c[2 * l : 2 * l + 1, cut[a]], ref.tilt_c[2 * l + 1 : 2 * l + 2, cut[a]]
            wide = jnp.concatenate([rc] * (quarter // lanes), 1), jnp.concatenate([rs] * (quarter // lanes), 1)
            er = wide[0] * cc - wide[1] * cs
            ei = sign * (wide[0] * cs + wide[1] * cc)
            re, im = value
            return re * er - im * ei, re * ei + im * er

        outgoing = []
        if kind == "enter":
            outgoing = [[]]
            for c in cut:
                phase = ref.slab[0, here, c]
                cosine, sine = jnp.cos(phase), jnp.sin(phase)
                ref.tr0[0, here, c] = cosine
                ref.tr0[1, here, c] = sine
                outgoing[0].append((cosine, sine))
        elif kind == "forward" or kind == "forward_band":
            for l in range(count):
                at = pl.ds(pl.multiple_of(l * rows + base_row, step), step)
                blocks = []
                for a, c in enumerate(cut):
                    tr, ti = ref.tr[0, here, c], ref.tr[1, here, c]
                    re, im = fields[l][a]
                    re, im = re * tr - im * ti, re * ti + im * tr
                    ref.passed[0, at, c] = re
                    ref.passed[1, at, c] = im
                    blocks.append((re, im) if kind == "forward" else tilt(l, a, (re, im), 1.0))
                outgoing.append(blocks)
        elif kind == "stats":
            adds = [0.0] * spec.stat_rows
            for a, c in enumerate(cut):
                power = []
                for l in range(count):
                    at = pl.ds(pl.multiple_of(l * rows + base_row, step), step)
                    re, im = fields[l][a]
                    ref.passed[0, at, c] = re
                    ref.passed[1, at, c] = im
                    power.append(re * re + im * im)
                values = list(power)
                for l in range(count):
                    for m in range(l, count):
                        values.append(power[l] * power[m])
                seen = [ref.measured[p, here, c].astype(f32) for p in range(spec.patterns)]
                for p in range(spec.patterns):
                    for l in range(count):
                        values.append(seen[p] * power[l])
                values += seen
                for k, value in enumerate(values):
                    adds[k] = adds[k] + fold(value)
            return tuple(x + y for x, y in zip(carry, adds))
        elif kind == "weigh":
            outgoing = [[] for _ in range(count)]
            for a, c in enumerate(cut):
                camera, power = [], []
                for l in range(count):
                    at = pl.ds(pl.multiple_of(l * rows + base_row, step), step)
                    re, im = ref.passed[0, at, c], ref.passed[1, at, c]
                    camera.append((re, im))
                    power.append(re * re + im * im)
                weight = [0.0] * count
                for p in range(spec.patterns):
                    lit = sum(code[p][l] * power[l] for l in range(count))
                    seen = ref.measured[p, here, c].astype(f32)
                    misfit = lit * (1.0 / power_mean[p]) - seen * (1.0 / count_mean[p])
                    pull = (misfit - couple[p]) * (1.0 / power_mean[p])
                    for l in range(count):
                        weight[l] = weight[l] + code[p][l] * pull
                for l in range(count):
                    scale = 2.0 * weight[l]
                    outgoing[l].append((scale * camera[l][0], scale * camera[l][1]))
        elif kind == "back" or kind == "back_band":
            grads = [0.0] * 4
            for l in range(count):
                at = pl.ds(pl.multiple_of(l * rows + base_row, step), step)
                blocks = []
                for a, c in enumerate(cut):
                    re, im = fields[l][a]
                    if kind == "back_band":
                        re, im = tilt(l, a, (re, im), -1.0)
                    pr, pi = ref.passed[0, at, c], ref.passed[1, at, c]
                    grads[a] = grads[a] + (pr * im - pi * re)
                    tr, ti = ref.tr[0, here, c], ref.tr[1, here, c]
                    blocks.append((re * tr + im * ti, im * tr - re * ti))
                outgoing.append(blocks)
            for a, c in enumerate(cut):
                ref.grad[here, c] = grads[a]
        elif kind == "leave":
            for a, c in enumerate(cut):
                tr, ti = ref.tr[0, here, c], ref.tr[1, here, c]
                re, im = fields[0][a]
                ref.grad[here, c] = tr * im - ti * re
        for l, blocks in enumerate(outgoing):
            at = pl.ds(pl.multiple_of(l * rows + base_row, step), step)
            for j, (re, im) in enumerate(row_spread(blocks, twiddle)):
                high, low = split(re)
                hi[j, at, :quarter] = high
                lo[j, at, :quarter] = low
                high, low = split(im)
                hi[j, at, quarter:] = high
                lo[j, at, quarter:] = low
        return carry

    if kind == "stats":
        stats = lax.fori_loop(0, rows // step, chunk, tuple(stats))
        packed = [jnp.sum(row, 0, keepdims=True) for row in stats]
        packed.append(jnp.zeros((ref.stage.shape[0] - len(packed), lanes), f32))
        packed = jnp.concatenate(packed, 0)
        ref.stage[...] = packed
        pl.semaphore_wait(barrier, devs - 1)
        send_all(ref, me, devs)
        finish(ref, me, devs)
        return
    lax.fori_loop(0, rows // step, chunk, 0)
    if not sends:
        return
    pl.semaphore_wait(barrier, devs - 1)

    def emit(j):
        y = dot3((hi[j, :total, :], lo[j, :total, :]), (ref.fwd[0], ref.fwd[1]))
        if spec.target == "full":
            for q in range(per):
                ref.stage[per * j + q] = y[:, q * lanes : (q + 1) * lanes].reshape(count, rows, lanes)
        else:
            flipped = y.T
            deep = flipped.shape[0] // per
            for q in range(per):
                ref.stage[per * j + q] = flipped[q * deep : (q + 1) * deep]
        for q in range(per):
            send(ref, me, per * j + lax.rem(me + q, per))

    for j in groups(me, per):
        emit(j)
    if kind == "enter":
        pupil_out(spec, ref, me)
        prepare(spec, ref, me)
        pupil_in(spec, ref, me)
    finish(ref, me, devs)


def pupil_copy(spec, ref, j, dest):
    return pltpu.make_async_remote_copy(
        src_ref=ref.own.at[j], dst_ref=ref.pupil, send_sem=ref.psent.at[j], recv_sem=ref.pgot,
        device_id=dict(pat=dest), device_id_type=pl.DeviceIdType.MESH,
    )


def pupil_out(spec, ref, me):
    per = spec.devs // 4
    for q in range(per):

        @pl.when(me == spec.owners[q])
        def _():
            for j in range(4):
                pupil_copy(spec, ref, j, per * j + q).start()


def pupil_in(spec, ref, me):
    per = spec.devs // 4
    pupil_copy(spec, ref, 0, partner(me, 1, spec.devs)).wait_recv()
    for q in range(per):

        @pl.when(me == spec.owners[q])
        def _():
            for j in range(4):
                pupil_copy(spec, ref, j, per * j + q).wait_send()


def prepare(spec, ref, me):
    size, quarter = 4 * spec.quarter, spec.quarter
    per, half, step = spec.devs // 4, lanes // 2, 16
    cutoff = size // 2 * (size // 2)

    def phases(i, carry):
        here = pl.ds(pl.multiple_of(i * step, step), step)
        for s, out in ((1, ref.tr1), (2, ref.tr2)):
            phase = ref.slab[s, here, :]
            out[0, here, :] = jnp.cos(phase)
            out[1, here, :] = jnp.sin(phase)
        return carry

    lax.fori_loop(0, spec.rows // step, phases, 0)

    def centred(index):
        return jnp.where(index >= size // 2, index - size, index)

    def spectrum(i, carry):
        here = pl.ds(pl.multiple_of(i * step, step), step)
        row = lax.broadcasted_iota(jnp.int32, (step, lanes), 0) + i * step
        lane = lax.broadcasted_iota(jnp.int32, (step, lanes), 1)
        lane = jnp.where(lane < half, lane, lane - half)
        col = 4 * (lax.rem(me, per) * half + lane) + me // per
        for l in range(spec.leds):
            v = centred(col + ref.freq[l, 1])
            for j in range(4):
                u = centred(4 * row + j + ref.freq[l, 0])
                radius = u * u + v * v
                inside = radius <= cutoff
                height = jnp.sqrt(jnp.maximum(cutoff - radius, 0).astype(f32))
                shift = spread_rate * (height - float(size // 2))
                ref.prop[0, l, j, here, :] = jnp.where(inside, jnp.cos(shift), 0.0)
                ref.prop[1, l, j, here, :] = jnp.where(inside, jnp.sin(shift), 0.0)
        return carry

    lax.fori_loop(0, quarter // step, spectrum, 0)


def run_rows(channel, kind, source, target, dims, inputs, outputs):
    spec = Names(**vars(dims), kind=kind, source=source, target=target)
    count = spec.count
    total = count * spec.rows
    wide = 2 * spec.quarter
    names = list(inputs) + list(outputs) + ["hi", "lo", "zs"]
    sends = "y" in outputs
    comm = []
    if sends:
        names += ["stage", "sent", "got", "kept"]
        shape = outputs["y"]
        comm = comm_scratch(shape[1:] if kind == "stats" else shape, spec.devs)
    if kind == "enter":
        names += ["psent", "pgot"]
        comm += [pltpu.SemaphoreType.DMA((4,)), pltpu.SemaphoreType.DMA]
    spec.names = names
    vmem = pl.BlockSpec(memory_space=pltpu.VMEM)
    in_specs = [
        pl.BlockSpec(memory_space=pltpu.SMEM) if name in ("code", "freq") else vmem for name in inputs
    ]
    return pl.pallas_call(
        functools.partial(row_kernel, spec),
        out_shape=[jax.ShapeDtypeStruct(shape, f32) for shape in outputs.values()],
        in_specs=in_specs,
        out_specs=[anywhere if name in ("y", "pupil") else vmem for name in outputs],
        scratch_shapes=[
            pltpu.VMEM((4, total, wide), bf16),
            pltpu.VMEM((4, total, wide), bf16),
            pltpu.VMEM((4, total, wide), f32),
        ]
        + comm,
        compiler_params=comm_params(channel) if sends else None,
        name="rows_" + kind,
    )(*inputs.values())


def col_kernel(spec, x_ref, p_ref, w_ref, t_ref, y_ref, hi, lo, zs, stage, sent, got, kept):
    ref = Names(y=y_ref, stage=stage, sent=sent, got=got, kept=kept, same=False)
    me, barrier = greet(spec.devs)
    rows, quarter, devs = spec.rows, spec.quarter, spec.devs
    count_in, count_out, sign = spec.count_in, spec.count_out, spec.sign
    count = p_ref.shape[1]
    per = devs // 4
    weights = (w_ref[0], w_ref[1])
    wide_out = count_out * lanes

    def spread(l):
        at = slice(l * lanes, (l + 1) * lanes)

        def step(i, carry):
            here = pl.ds(pl.multiple_of(i * rows, rows), rows)
            x0, x1, x2, x3 = [x_ref[per * a + i, l] for a in range(4)]
            s, t, d, e = x0 + x2, x1 + x3, x0 - x2, turn(x1 - x3)
            for j, value in enumerate((s + t, d + e, s - t, d - e)):
                if j:
                    value = value * t_ref[0, j - 1, here, :] + turn(value) * t_ref[1, j - 1, here, :]
                high, low = split(value)
                hi[j, here, at] = high
                lo[j, here, at] = low
            return carry

        lax.fori_loop(0, per, step, 0)

    def spectra(first, number):
        span = slice(first * lanes, (first + number) * lanes)
        found = []
        for j in range(4):
            y = dot3(weights, (hi[j, :, span], lo[j, :, span]))
            found.append([])
            for l in range(number):
                at = slice(l * lanes, (l + 1) * lanes)
                found[j].append(y[:quarter, at] + turn(y[quarter:, at]))
        return found

    def pass_on(l, fields):
        at = slice(l * lanes, (l + 1) * lanes)
        for j in range(4):
            high, low = split(fields[j])
            hi[j, :, at] = high
            lo[j, :, at] = low
        for j in range(4):
            y = dot3(weights, (hi[j, :, at], lo[j, :, at]))
            value = y[:quarter] - turn(y[quarter:])
            if j:
                value = value * t_ref[0, j - 1] - turn(value) * t_ref[1, j - 1]
            zs[j, :, at] = value
        if l == 0:
            pl.semaphore_wait(barrier, devs - 1)

        def gather(step, carry):
            i = lax.rem(me + step, per)
            here = pl.ds(pl.multiple_of(i * rows, rows), rows)
            g0, g1, g2, g3 = [zs[j, here, at] for j in range(4)]
            s, t, d, e = g0 + g2, g1 + g3, g0 - g2, turn(g1 - g3)
            for a, value in enumerate((s + t, d - e, s - t, d + e)):
                stage[per * a + i, l] = value
            return carry

        lax.fori_loop(0, per, gather, 0)
        send_all(ref, me, devs, l)

    def shaped(z, l, j):
        return z * p_ref[0, l, j] - sign * (turn(z) * p_ref[1, l, j])

    if count_in == count_out:
        for l in range(count):
            spread(l)
            z = spectra(l, 1)
            pass_on(l, [shaped(z[j][0], l, j) for j in range(4)])
    else:
        for l in range(count_in):
            spread(l)
        z = spectra(0, count_in)
        if count_out == 1:
            pass_on(0, [sum(shaped(z[j][l], l, j) for l in range(count)) for j in range(4)])
        else:
            for j in range(4):
                zs[j, :, wide_out:] = z[j][0]
            for l in range(count):
                pass_on(l, [shaped(zs[j, :, wide_out:], l, j) for j in range(4)])
    finish(ref, me, devs, tuple(range(count_out)))


def run_cols(channel, x, prop, tables, dims, count_in, count_out, sign):
    spec = Names(**vars(dims), count_in=count_in, count_out=count_out, sign=sign)
    rows, quarter, devs = dims.rows, dims.quarter, dims.devs
    wide = max(count_in, count_out) * lanes
    vmem = pl.BlockSpec(memory_space=pltpu.VMEM)
    return pl.pallas_call(
        functools.partial(col_kernel, spec),
        out_shape=jax.ShapeDtypeStruct((devs, count_out, rows, lanes), f32),
        in_specs=[vmem] * 4,
        out_specs=anywhere,
        scratch_shapes=[
            pltpu.VMEM((4, quarter, wide), bf16),
            pltpu.VMEM((4, quarter, wide), bf16),
            pltpu.VMEM((4, quarter, wide + lanes), f32),
        ]
        + comm_scratch((devs, count_out, rows, lanes), devs, count_out),
        compiler_params=comm_params(channel),
        name="cols",
    )(x, prop, jnp.asarray(tables.both), jnp.asarray(tables.twiddle))


def band_kernel(spec, x_ref, p_ref, w_ref, v_ref, y_ref, stage, sent, got, kept):
    ref = Names(y=y_ref, stage=stage, sent=sent, got=got, kept=kept, same=False)
    me, barrier = greet(spec.devs)
    devs, sign, count = spec.devs, spec.sign, spec.count
    half = lanes // 2
    lane = lax.broadcasted_iota(jnp.int32, x_ref.shape[1:], 1)
    pieces = [[], []]
    for s in range(0, devs, 2):
        even, odd = x_ref[s], x_ref[s + 1]
        pieces[0].append(jnp.where(lane < half, even, pltpu.roll(odd, half, 1)))
        pieces[1].append(jnp.where(lane < half, pltpu.roll(even, half, 1), odd))
    field = jnp.concatenate([jnp.concatenate(p, 1) for p in pieces], 0)
    wide = w_ref.shape[2] // 2
    deep = v_ref.shape[2] // 2
    cols = x_ref.shape[1] // 2
    both = dot3(split(field), (w_ref[0], w_ref[1]))
    scaled = []
    for l in range(count):
        re = slice(2 * l * cols, (2 * l + 1) * cols)
        im = slice((2 * l + 1) * cols, (2 * l + 2) * cols)
        yr = both[re, :wide] + both[im, wide:]
        yi = both[im, :wide] - both[re, wide:]
        pr, pi = p_ref[0], sign * p_ref[1]
        scaled += [yr * pr - yi * pi, yr * pi + yi * pr]
    both = dot3(split(jnp.concatenate(scaled, 0)), (v_ref[0], v_ref[1]))
    out = []
    for l in range(count):
        re = slice(2 * l * cols, (2 * l + 1) * cols)
        im = slice((2 * l + 1) * cols, (2 * l + 2) * cols)
        out.append(
            jnp.concatenate(
                [both[re, :deep] - both[im, deep:], both[im, :deep] + both[re, deep:]], 0
            )
        )
    for s in range(0, devs, 2):
        at = slice(s * half, s * half + lanes)
        first, second = out[0][:, at], out[1][:, at]
        stage[s] = jnp.where(lane < half, first, pltpu.roll(second, half, 1))
        stage[s + 1] = jnp.where(lane < half, pltpu.roll(first, half, 1), second)
    pl.semaphore_wait(barrier, devs - 1)
    send_all(ref, me, devs)
    finish(ref, me, devs)


def run_band(channel, x, pupil, tables, dims, sign):
    vmem = pl.BlockSpec(memory_space=pltpu.VMEM)
    return pl.pallas_call(
        functools.partial(band_kernel, Names(**vars(dims), sign=sign)),
        out_shape=jax.ShapeDtypeStruct(x.shape, f32),
        in_specs=[vmem] * 4,
        out_specs=anywhere,
        scratch_shapes=comm_scratch(x.shape, dims.devs),
        compiler_params=comm_params(channel),
        name="pupil_cols",
    )(x, pupil, jnp.asarray(tables.band), jnp.asarray(tables.band_inv))


def body(slab_phase, pupil_phase, pupil_mask, led_code, led_freq, measured):
    devs = lax.axis_size("pat")
    position = lax.axis_index("pat")
    slab_count, rows, size = slab_phase.shape
    patterns, count = led_code.shape
    quarter, cols, per = size // 4, size // devs, devs // 4
    band = 2 * pupil_radius
    band_cols = band // devs
    dims = Names(
        count=count, rows=rows, quarter=quarter, devs=devs, patterns=patterns,
        area=float(size * size),
    )
    rt = row_tables(size, cols, band_cols)
    ct = col_tables(size)
    shape_full = (devs, count, rows, lanes)
    shape_band = (devs, 2 * band_cols, count * rows)
    shape_field = (2, count * rows, size)
    twiddle, table = rt.twiddle, rt

    def near(x):
        return jnp.concatenate([x[:, size - pupil_radius :], x[:, :pupil_radius]], 1)

    opening, phase = near(pupil_mask).astype(f32), near(pupil_phase)
    own = jnp.stack([opening * jnp.cos(phase), opening * jnp.sin(phase)])
    own = jnp.transpose(own.reshape(2, cols // 4, 4, band), (2, 0, 1, 3))
    owners = [(q - pupil_radius // cols) % devs for q in range(per)]

    def wave(freq, index):
        turns = (freq[:, None] * index[None, :]) % size
        angle = turns.astype(f32) * (2.0 * math.pi / size)
        return jnp.stack([jnp.cos(angle), jnp.sin(angle)], 1).reshape(2 * count, -1)

    tilt_c = wave(led_freq[:, 1], jnp.arange(size, dtype=jnp.int32))
    tilt_r = wave(led_freq[:, 0], position * rows + jnp.arange(rows, dtype=jnp.int32))
    tilt_r = jnp.broadcast_to(tilt_r[:, :, None], (2 * count, rows, lanes))
    tilts = dict(tilt_r=tilt_r, tilt_c=tilt_c)
    full_both = dict(inv=table.full_inv, fwd=table.full, twiddle=twiddle)

    one = Names(**{**vars(dims), **dict(count=1)}, leds=count, owners=owners)
    shape_trans = (2, rows, size)
    y, tr0, tr1, tr2, prop, pupil = run_rows(
        7, "enter", None, "full", one,
        dict(slab=slab_phase, own=own, freq=led_freq, fwd=table.full, twiddle=twiddle),
        dict(
            y=(devs, 1, rows, lanes), tr0=shape_trans, tr1=shape_trans, tr2=shape_trans,
            prop=(2, count, 4, quarter, lanes), pupil=(2, band_cols, band),
        ),
    )
    transmission = [tr0, tr1, tr2]
    x = run_cols(1, y, prop, ct, dims, 1, count, 1.0)
    y, passed1 = run_rows(
        8, "forward", "full", "full", dims, dict(x=x, tr=transmission[1], **full_both),
        dict(y=shape_full, passed=shape_field),
    )
    x = run_cols(2, y, prop, ct, dims, count, count, 1.0)
    y, passed2 = run_rows(
        9, "forward_band", "full", "band", dims,
        dict(x=x, tr=transmission[2], inv=table.full_inv, fwd=table.band, twiddle=twiddle, **tilts),
        dict(y=shape_band, passed=shape_field),
    )
    x = run_band(3, y, pupil, ct, dims, 1.0)
    stat_rows = count + count * (count + 1) // 2 + patterns * count + patterns
    dims.stat_rows = stat_rows
    camera, sums = run_rows(
        10, "stats", "band", None, dims,
        dict(x=x, inv=table.band_inv, twiddle=twiddle, measured=measured),
        dict(passed=shape_field, y=(devs, -(-stat_rows // 8) * 8, lanes)),
    )
    (y,) = run_rows(
        11, "weigh", None, "band", dims,
        dict(stats=sums, code=led_code, passed=camera, measured=measured, fwd=table.band, twiddle=twiddle),
        dict(y=shape_band),
    )
    x = run_band(4, y, pupil, ct, dims, -1.0)
    y, grad2 = run_rows(
        12, "back_band", "band", "full", dims,
        dict(x=x, tr=transmission[2], passed=passed2, inv=table.band_inv, fwd=table.full, twiddle=twiddle, **tilts),
        dict(y=shape_full, grad=(rows, size)),
    )
    x = run_cols(5, y, prop, ct, dims, count, count, -1.0)
    y, grad1 = run_rows(
        13, "back", "full", "full", dims,
        dict(x=x, tr=transmission[1], passed=passed1, **full_both),
        dict(y=shape_full, grad=(rows, size)),
    )
    x = run_cols(6, y, prop, ct, dims, count, 1, -1.0)
    (grad0,) = run_rows(
        14, "leave", "full", None, one,
        dict(x=x, tr=transmission[0], inv=table.full_inv, twiddle=twiddle),
        dict(grad=(rows, size)),
    )
    return jnp.stack([grad0, grad1, grad2])


def solution(mesh):
    in_specs = (
        P("tiles", "pat", None),
        P("pat", None),
        P("pat", None),
        P(),
        P(),
        P("tiles", "pat", None),
    )
    out_specs = P("tiles", "pat", None)
    def run(slab_phase, *others):
        devs = mesh.shape["pat"]
        size, count = slab_phase.shape[-1], others[2].shape[1]
        fits = 2 * size == lanes * devs and count * size == lanes * devs and slab_phase.shape[0] == 3 * mesh.shape["tiles"]
        inner = body if fits else plain_body
        return jax.shard_map(inner, mesh=mesh, in_specs=in_specs, out_specs=out_specs, check_vma=False)(
            slab_phase, *others
        )

    return run
```
